32 devices in a mesh: px: 8 (over z, x), py: 4 (over y, core).
Axes of the slice: x: 2, y: 2, z: 4, core: 2. Of those that a mesh axis runs over, the one named last changes fastest.
Arguments:
- conserved: float32 [2, 2, 2, 2, 32, 32, 128], P(None, None, None, None, 'px', 'py'), may hold values from 0.075 to 36
- velocity: float32 [3, 3, 3, 3, 32, 32, 128], P(None, None, None, None, 'px', 'py'), may hold values from -6 to 6
- targets: float32 [2], replicated, may hold values from 0.5 to 2
- handoff_blocks: int32 [8, 32], P('px', 'py'), may hold values from 0 to 31, as said below
- handoff_owner: int32 [8, 32, 1], P('px', 'py'), may hold values from 0 to 3; in each aligned block of 8 rows (0 to 7, 8 to 15, ..., all dimensions but the last counted through in order) at most 4 rows name the same one
Outputs:
- fixed_state: float32 [2, 2, 2, 2, 32, 32, 128], P(None, None, None, None, 'px', 'py')
- handed: float32 [8, 64, 16, 128], P('px', 'py')
The draws below stay inside these ranges and needn't reach their ends.
Inputs may be any that keep to these rules, and one draw needn't show every extreme that they name: `handoff_blocks`: within one device's 8 entries the column numbers are distinct; column b is the local zone column (b // 8, b % 8). `handoff_owner`: owners are indices along py within the same px group; at most 4 of one device's entries name the same owner, and in some device one owner is named exactly 4 times.
All inputs are finite; a program needn't handle non-finite values.
Results may differ from the reference program's by a relative error of at most 0.00035.
Values sent between devices are 32-bit elements; how exact they have to be, the bound alone decides.
No kernel may reach another device: no remote copies, remote signals or barrier semaphores. Data moves between devices by JAX's collectives and lax.ppermute only.
A program may use at most 64 MiB of HBM per device.

```python
import math
import jax
import jax.numpy as jnp
import numpy as np
from jax import lax

CX = 4
CY = 8
NZ = 128
NH = 8
NX = 32
NY = 32
CAP = 4
N_PX = 8
N_PY = 4


def draw_conserved(key, part):
    key_one = jax.random.fold_in(jax.random.fold_in(key, 11), 0)
    key_level = jax.random.fold_in(key, 13)
    layout = (2, 2, 2, 2, NX, NY, NZ)
    profile = 1.0 + 2.0 * jnp.arange(NX, dtype=jnp.float32) / (NX - 1)
    block_level = jnp.exp(jax.random.uniform(key_level, (2, 1, 1, 1, N_PX, 1, 1), jnp.float32, math.log(0.5), math.log(2.0)))
    level_rows = jnp.repeat(block_level, CX, axis=4)
    spread_draw = jnp.exp(jax.random.uniform(key_one, layout, jnp.float32, math.log(0.5), math.log(2.0)))
    return spread_draw * profile[:, None, None] * level_rows


def draw_velocity(key, part):
    noise_key = jax.random.fold_in(key, 37)
    layout = (3, 3, 3, 3, NX, NY, NZ)
    noise = jax.random.truncated_normal(noise_key, -5.5, 5.5, layout, jnp.float32)
    offsets = 0.5 - jnp.array([0.0, 0.5, 1.0], jnp.float32)
    squeeze = jnp.stack([jnp.broadcast_to(offsets.reshape(3, 1, 1), (3, 3, 3)), jnp.broadcast_to(offsets.reshape(1, 3, 1), (3, 3, 3)), jnp.broadcast_to(offsets.reshape(1, 1, 3), (3, 3, 3))])
    return noise + squeeze[:, :, :, :, None, None, None]


def draw_handoff_blocks(key, part):
    device_count = N_PX * N_PY
    columns = CX * CY
    scores = jax.random.randint(jax.random.fold_in(key, 23), (device_count, columns), 0, 1 << 20) * columns + jnp.arange(columns, dtype=jnp.int32)
    chosen = jnp.argsort(scores, axis=1)[:, :NH].astype(jnp.int32)
    return chosen.reshape(N_PX, N_PY * NH)


def deal_out(key, own, number, rows, amount, top, most, lean):
    sequence = jax.random.permutation(key, amount)
    crowded, ordinary = shares(amount, rows * top, most, lean, True), shares(amount, rows * top, most, lean, False)
    places = jnp.arange(amount)

    def named(tallies, rotation):
        used = int((tallies > 0).sum())
        fixed = max(1, used // 4)
        moved = fixed + (places - fixed + rotation * (used - fixed)) % max(1, amount - fixed)
        return jnp.zeros((amount,), jnp.int32).at[sequence[jnp.where(places < fixed, places, moved)]].set(jnp.asarray(tallies, jnp.int32))

    tallies = jnp.where(number % 4 == 0, named(crowded, number // 4), named(ordinary, number - number // 4 - 1))
    mixed = jax.random.permutation(jax.random.fold_in(own, 3), amount)
    source_of, sink = mixed[0:amount // 2 * 2:2], mixed[1:amount // 2 * 2:2]
    slack = jnp.minimum(tallies[source_of] - 1, most - tallies[sink]) // 2
    slack = jnp.where((source_of == sequence[0]) | (sink == sequence[0]) | (tallies[sink] == 0), 0, jnp.maximum(slack, 0))
    moved = jax.random.randint(jax.random.fold_in(own, 4), (amount // 2,), 0, 1 << 20) % (slack + 1)
    tallies = tallies.at[source_of].add(-moved).at[sink].add(moved)
    members = jnp.searchsorted(jnp.cumsum(tallies), jnp.arange(rows * top), side="right").astype(jnp.int32)
    grid = members.reshape(top, rows).T
    grid = grid[jax.random.permutation(jax.random.fold_in(own, 1), rows)]
    rotation = jax.random.randint(jax.random.fold_in(own, 2), (rows, 1), 0, top)
    return jnp.take_along_axis(grid, (jnp.arange(top)[None, :] + rotation) % top, axis=1)


def shares(number_of, total, limit, slope, full):
    weights = [(1 << 20) // math.isqrt(standing ** slope) + 1 for standing in range(1, number_of + 1)]
    largest = limit if full else min(limit, max(-(-total // number_of), total * weights[0] // sum(weights)))
    least = 1 if total - largest >= number_of - 1 else 0
    counts, spare = [largest] + [least] * (number_of - 1), total - largest - least * (number_of - 1)
    while spare > 0:
        free = [i for i in range(1, number_of) if counts[i] < largest] or [i for i in range(1, number_of) if counts[i] < limit]
        mass, budget = sum([weights[i] for i in free]), spare
        for i in free:
            extra = min(limit - counts[i], max(1, budget * weights[i] // mass), spare)
            counts[i] = counts[i] + extra
            spare = spare - extra
    return np.array(counts)


def setup_inputs(seed: int = 0) -> dict:
    keys = jax.random.split(jax.random.key(seed), 6)
    conserved = draw_conserved(jax.random.fold_in(keys[5], 71), 0)
    velocity = draw_velocity(jax.random.fold_in(keys[5], 71), 0)
    targets = jnp.clip(jax.random.uniform(keys[2], (2,), jnp.float32, 0.5, 2.0), 0.5, 2.0)
    handoff_blocks = draw_handoff_blocks(jax.random.fold_in(keys[5], 71), 0)
    handoff_owner_keys = jax.random.split(jax.random.fold_in(keys[4], 1), N_PX * (N_PY * NH) // NH)
    handoff_owner_turns = jax.random.permutation(jax.random.fold_in(keys[4], 3), N_PX * (N_PY * NH) // NH)
    handoff_owner = jax.vmap(lambda own, number: deal_out(jax.random.fold_in(keys[4], 2), own, number, NH, N_PY, 1, CAP, 2))(handoff_owner_keys, handoff_owner_turns).reshape((N_PX, N_PY * NH, 1))
    return {"conserved": conserved, "velocity": velocity, "targets": targets, "handoff_blocks": handoff_blocks, "handoff_owner": handoff_owner}


gamma_less = 0.4
force_step = 0.02
advect_step = 0.5
highest = lax.Precision.HIGHEST

def triple(factor_one, factor_two, factor_three):
    return np.kron(np.kron(factor_one, factor_two), factor_three)

def build_tables():
    offset = 0.5 / math.sqrt(3.0)
    gauss_nodes = np.array([0.5 - offset, 0.5 + offset])
    linear = np.stack([1.0 - gauss_nodes, gauss_nodes], 1)
    quadratic = np.stack([2.0 * (gauss_nodes - 0.5) * (gauss_nodes - 1.0), -4.0 * gauss_nodes * (gauss_nodes - 1.0), 2.0 * gauss_nodes * (gauss_nodes - 0.5)], 1)
    slopes = np.stack([4.0 * gauss_nodes - 3.0, 4.0 - 8.0 * gauss_nodes, 4.0 * gauss_nodes - 1.0], 1)
    line_mass = np.array([[1.0 / 3.0, 1.0 / 6.0], [1.0 / 6.0, 1.0 / 3.0]])
    line_inverse = np.array([[4.0, -2.0], [-2.0, 4.0]])
    line_drift = np.array([[-0.5, -0.5], [0.5, 0.5]])
    basis = triple(linear, linear, linear)
    gradient = np.stack([triple(slopes, quadratic, quadratic), triple(quadratic, slopes, quadratic), triple(quadratic, quadratic, slopes)], 1).reshape(8, 81)
    inverse = triple(line_inverse, line_inverse, line_inverse)
    project = inverse @ basis.T / 8.0
    stiffness = np.stack([triple(line_drift, line_mass, line_mass), triple(line_mass, line_drift, line_mass), triple(line_mass, line_mass, line_drift)])
    face_mass = np.kron(line_mass, line_mass)
    return tuple((jnp.asarray(entry_table, jnp.float32) for entry_table in (basis, gradient, inverse, project, stiffness, face_mass)))

def face_weight(fluxes, face_mass):
    layout = fluxes.shape
    grouped = fluxes.reshape(layout[0], 4, -1)
    return jnp.einsum('ab,fbn->fan', face_mass, grouped, precision=highest).reshape(layout)

def upwind(left_trace, right_trace, speeds, face_mass):
    fluxes = 0.5 * speeds * (left_trace + right_trace) + 0.5 * jnp.abs(speeds) * (left_trace - right_trace)
    return face_weight(fluxes, face_mass)

def lagrange_section(conserved, velocity, tables):
    basis, gradient, inverse, project, stiffness, face_mass = tables
    layout = conserved.shape
    zone_count = layout[4] * layout[5] * layout[6]
    fields = conserved.reshape(2, 8, zone_count)
    node_motion = velocity.reshape(81, zone_count)
    divergence = jnp.dot(gradient, node_motion, precision=highest)
    pressure = gamma_less * jnp.dot(basis, fields[1], precision=highest)
    energy = fields[1] - force_step * jnp.dot(project, pressure * divergence, precision=highest)
    lagrange = jnp.stack([fields[0], energy]).reshape(layout)
    mean_motion = lax.optimization_barrier(jnp.sum(velocity.reshape(3, 27, layout[4], layout[5], layout[6]), axis=1)) / 27.0
    padded = jnp.pad(mean_motion, ((0, 0), (0, 0), (0, 0), (1, 1)))
    relaxed = 0.25 * (padded[..., :-2] + 2.0 * mean_motion + padded[..., 2:])
    return (lagrange, mean_motion - relaxed)

def advect(lagrange, relative, x_faces, y_faces, tables):
    basis, gradient, inverse, project, stiffness, face_mass = tables
    layout = lagrange.shape
    zone_count = layout[4] * layout[5] * layout[6]
    flat_state = lagrange.reshape(2, 8, zone_count)
    volume = jnp.zeros_like(flat_state)
    for direction in range(3):
        volume = volume + jnp.einsum('jk,fkn->fjn', stiffness[direction], flat_state, precision=highest) * relative[direction].reshape(1, 1, zone_count)
    flux_x = upwind(x_faces[0], x_faces[1], x_faces[2], face_mass)
    face_x = jnp.stack([-flux_x[:, :, :, :-1], flux_x[:, :, :, 1:]], axis=1)
    flux_y = upwind(y_faces[0], y_faces[1], y_faces[2], face_mass)
    face_y = jnp.stack([-flux_y[:, :, :, :, :-1], flux_y[:, :, :, :, 1:]], axis=2)
    padded_z = jnp.pad(lagrange, ((0, 0),) * 6 + ((1, 1),))
    motion_z = jnp.pad(relative[2], ((0, 0), (0, 0), (1, 1)))
    flux_z = upwind(padded_z[:, :, :, 1, :, :, :-1], padded_z[:, :, :, 0, :, :, 1:], 0.5 * (motion_z[..., :-1] + motion_z[..., 1:]), face_mass)
    face_z = jnp.stack([-flux_z[..., :-1], flux_z[..., 1:]], axis=3)
    balance = volume - (face_x + face_y + face_z).reshape(2, 8, zone_count)
    remapped = flat_state + advect_step * jnp.einsum('jk,fkn->fjn', inverse, balance, precision=highest)
    return remapped.reshape(layout)

def reference(conserved, velocity, targets, handoff_blocks, handoff_owner):
    tables = build_tables()
    lagrange, relative = lagrange_section(conserved, velocity, tables)
    padded_x = jnp.pad(lagrange, ((0, 0),) * 4 + ((1, 1), (0, 0), (0, 0)))
    motion_x = jnp.pad(relative[0], ((1, 1), (0, 0), (0, 0)))
    x_faces = (padded_x[:, 1, :, :, :-1], padded_x[:, 0, :, :, 1:], 0.5 * (motion_x[:-1] + motion_x[1:]))
    padded_y = jnp.pad(lagrange, ((0, 0),) * 5 + ((1, 1), (0, 0)))
    motion_y = jnp.pad(relative[1], ((0, 0), (1, 1), (0, 0)))
    y_faces = (padded_y[:, :, 1, :, :, :-1], padded_y[:, :, 0, :, :, 1:], 0.5 * (motion_y[:, :-1] + motion_y[:, 1:]))
    remapped = advect(lagrange, relative, x_faces, y_faces, tables)
    totals = lax.optimization_barrier(jnp.sum(remapped.reshape(2, -1), axis=1))
    field_means = totals / (8.0 * NX * NY * NZ)
    fixed_state = remapped * (targets / field_means).reshape(2, 1, 1, 1, 1, 1, 1)
    blocks = handoff_blocks.reshape(N_PX, N_PY, NH).astype(jnp.int32)
    owners = handoff_owner.reshape(N_PX, N_PY, NH).astype(jnp.int32)
    onehot = (owners[..., None] == jnp.arange(N_PY, dtype=jnp.int32)).astype(jnp.int32)
    earlier = (jnp.cumsum(onehot, axis=2) - onehot).astype(jnp.int32)
    slot_index = lax.optimization_barrier(jnp.sum(onehot * earlier, axis=3)).astype(jnp.int32)
    source = jnp.arange(N_PY, dtype=jnp.int32)[None, :, None]
    position = (owners * (N_PY * CAP) + source * CAP + slot_index).astype(jnp.int32)
    column_x = (jnp.arange(N_PX, dtype=jnp.int32)[:, None, None] * CX + blocks // CY).astype(jnp.int32)
    column_y = (source * CY + blocks % CY).astype(jnp.int32)
    block_rows = fixed_state.reshape(16, NX, NY, NZ)[:, column_x, column_y, :]
    block_rows = jnp.moveaxis(block_rows, 0, 3)
    row_px = jnp.broadcast_to(jnp.arange(N_PX, dtype=jnp.int32)[:, None, None], position.shape)
    handed = jnp.zeros((N_PX, N_PY * N_PY * CAP, 16, NZ), jnp.float32).at[row_px, position].set(block_rows)
    return (fixed_state, handed)
```

```python
import functools
import math

import jax
import jax.numpy as jnp
from jax import lax
from jax.experimental import pallas as pl
from jax.experimental.pallas import tpu as pltpu
from jax.sharding import PartitionSpec as P

gamma_less = 0.4
force_step = 0.02
gauss_offset = 0.5 / math.sqrt(3.0)


def in_vmem():
    return pl.BlockSpec(memory_space=pltpu.VMEM)


def in_place():
    return pl.BlockSpec(memory_space=pl.ANY)


def shape_of(*shape):
    return jax.ShapeDtypeStruct(shape, jnp.float32)


def kernel_options():
    return pltpu.CompilerParams(vmem_limit_bytes=16 * 1024 * 1024)


def paired(size, first):
    pairs = []
    for low in range(first, size - 1, 2):
        pairs += [(low, low + 1), (low + 1, low)]
    return pairs


def partner_of(index, hop, size):
    if size & (size - 1) == 0:
        return index ^ hop
    return lax.rem(index + hop, size)


def giver_of(index, hop, size):
    if size & (size - 1) == 0:
        return index ^ hop
    return lax.rem(index + size - hop, size)


def lifted(low, high, value):
    middle = 0.5 * (low + high)
    tilt = value * (low - high)
    return middle + tilt, middle - tilt


def along(values, direction, operation):
    stride = (4, 2, 1)[direction]
    out = [None] * 8
    for low in range(8):
        if not low & stride:
            out[low], out[low + stride] = operation(values[low], values[low + stride])
    return out


def quadratic_values(first, second, third):
    middle = (1.0 / 6.0) * (first + third) + (2.0 / 3.0) * second
    tilt = gauss_offset * (third - first)
    return middle - tilt, middle + tilt


def quadratic_slopes(first, second, third):
    rise = third - first
    bend = (4.0 * gauss_offset) * ((first + third) - 2.0 * second)
    return rise - bend, rise + bend


def lagrange_kernel(
    sizes,
    conserved_ref,
    velocity_ref,
    state_ref,
    relative_ref,
    xa_ref,
    xb_ref,
    ya_ref,
    yb_ref,
    motion_ref,
    state_sem,
    motion_sem,
):
    width_x, width_y, depth_z = sizes
    copies = []
    for x in range(width_x):
        copies.append(
            (
                pltpu.make_async_copy(
                    conserved_ref.at[:, x], state_ref.at[:, x], state_sem.at[x]
                ),
                pltpu.make_async_copy(
                    velocity_ref.at[:, x], motion_ref.at[:, x], motion_sem.at[x]
                ),
            )
        )
    for state_copy, motion_copy in copies:
        state_copy.start()
        motion_copy.start()
    lane = lax.broadcasted_iota(jnp.int32, (width_y, depth_z), 1)
    for x in range(width_x):
        copies[x][0].wait()
        copies[x][1].wait()
        divergence = [None] * 8
        for component in range(3):

            def node(a, b, c):
                return motion_ref[component * 27 + a * 9 + b * 3 + c, x]

            total = None
            stage = {}
            for a in range(3):
                for b in range(3):
                    line = [node(a, b, c) for c in range(3)]
                    part = (line[0] + line[1]) + line[2]
                    total = part if total is None else total + part
                    rule = quadratic_slopes if component == 2 else quadratic_values
                    stage[a, b, 0], stage[a, b, 1] = rule(*line)
            second = {}
            for a in range(3):
                for c in range(2):
                    rule = quadratic_slopes if component == 1 else quadratic_values
                    second[a, 0, c], second[a, 1, c] = rule(
                        stage[a, 0, c], stage[a, 1, c], stage[a, 2, c]
                    )
            for b in range(2):
                for c in range(2):
                    rule = quadratic_slopes if component == 0 else quadratic_values
                    pair = rule(second[0, b, c], second[1, b, c], second[2, b, c])
                    for a in range(2):
                        point = a * 4 + b * 2 + c
                        divergence[point] = (
                            pair[a] if component == 0 else divergence[point] + pair[a]
                        )
            mean = total * (1.0 / 27.0)
            before = jnp.where(lane == 0, 0.0, pltpu.roll(mean, 1, 1))
            after = jnp.where(lane == depth_z - 1, 0.0, pltpu.roll(mean, depth_z - 1, 1))
            relative_ref[component, x] = mean - 0.25 * ((before + 2.0 * mean) + after)
        energy = [state_ref[8 + corner, x] for corner in range(8)]
        work = energy
        for direction in range(3):
            work = along(work, direction, lambda p, q: lifted(p, q, gauss_offset))
        work = [(gamma_less * work[point]) * divergence[point] for point in range(8)]
        for direction in range(3):
            work = along(work, direction, lambda p, q: lifted(p, q, 3.0 * gauss_offset))
        for corner in range(8):
            state_ref[8 + corner, x] = energy[corner] - force_step * work[corner]
    odd_x = lax.rem(lax.axis_index("px"), 2)
    for out_ref, side in ((xa_ref, 1 - odd_x), (xb_ref, odd_x)):
        place = side * (width_x - 1)
        for field in range(2):
            for k in range(4):
                out_ref[field * 4 + k] = state_ref[field * 8 + side * 4 + k, place]
        out_ref[8] = relative_ref[0, place]
    odd_y = lax.rem(lax.axis_index("py"), 2)
    state_rows = state_ref.reshape(16 * width_x * width_y, depth_z)
    relative_rows = relative_ref.reshape(3 * width_x * width_y, depth_z)
    column = width_x * width_y
    for out_ref, side in ((ya_ref, 1 - odd_y), (yb_ref, odd_y)):
        place = side * (width_y - 1)
        for field in range(2):
            for a in range(2):
                for c in range(2):
                    start = (field * 8 + a * 4 + c) * column + side * 2 * column + place
                    out_ref[field * 4 + a * 2 + c] = state_rows[
                        pl.ds(start, width_x, stride=width_y), :
                    ]
        out_ref[8] = relative_rows[pl.ds(column + place, width_x, stride=width_y), :]


def lagrange_call(conserved, velocity):
    width_x, width_y, depth_z = conserved.shape[4:]
    sizes = (width_x, width_y, depth_z)
    return pl.pallas_call(
        functools.partial(lagrange_kernel, sizes),
        out_shape=(
            shape_of(16, *sizes),
            shape_of(3, *sizes),
            shape_of(9, width_y, depth_z),
            shape_of(9, width_y, depth_z),
            shape_of(9, width_x, depth_z),
            shape_of(9, width_x, depth_z),
        ),
        in_specs=[in_place()] * 2,
        out_specs=(in_vmem(),) * 6,
        scratch_shapes=[
            pltpu.VMEM((81,) + sizes, jnp.float32),
            pltpu.SemaphoreType.DMA((width_x,)),
            pltpu.SemaphoreType.DMA((width_x,)),
        ],
        compiler_params=kernel_options(),
        name="lagrange",
    )(conserved.reshape((16,) + sizes), velocity.reshape((81,) + sizes))


def remap_kernel(
    sizes,
    count_py,
    entries,
    capacity,
    state_ref,
    relative_ref,
    xa_ref,
    xb_ref,
    ya_ref,
    yb_ref,
    blocks_hbm,
    owners_hbm,
    targets_hbm,
    *refs,
):
    width_x, width_y, depth_z = sizes
    out_ref, total_ref, goal_ref = refs[:3]
    send_refs = refs[3 : 3 + count_py]
    sending, blocks_ref, owners_ref, targets_ref, sems = refs[3 + count_py :]
    copies = [
        pltpu.make_async_copy(blocks_hbm, blocks_ref, sems.at[0]),
        pltpu.make_async_copy(owners_hbm, owners_ref, sems.at[1]),
        pltpu.make_async_copy(targets_hbm, targets_ref, sems.at[2]),
    ]
    for copy in copies:
        copy.start()
    lane = lax.broadcasted_iota(jnp.int32, (width_y, depth_z), 1)
    row = lax.broadcasted_iota(jnp.int32, (width_y, depth_z), 0)
    even_x = lax.rem(lax.axis_index("px"), 2) == 0
    even_y = lax.rem(lax.axis_index("py"), 2) == 0

    def below_x(k):
        return jnp.where(even_x, xb_ref[k], xa_ref[k])

    def above_x(k):
        return jnp.where(even_x, xa_ref[k], xb_ref[k])

    def split(speed):
        return jnp.maximum(speed, 0.0), jnp.minimum(speed, 0.0)

    sending[...] = jnp.zeros(sending.shape, jnp.float32)
    totals = [None, None]
    speed = relative_ref[0, 0]
    coefficient = split(0.5 * (below_x(8) + speed))
    lower_x = [
        coefficient[0] * below_x(field * 4 + k) + coefficient[1] * state_ref[field * 8 + k, 0]
        for field in range(2)
        for k in range(4)
    ]
    for x in range(width_x):
        speed_x, speed_y, speed_z = (relative_ref[d, x] for d in range(3))
        beyond = above_x(8) if x == width_x - 1 else relative_ref[0, x + 1]
        upper_x_rate = split(0.5 * (speed_x + beyond))
        y_below = jnp.where(even_y, yb_ref[8, pl.ds(x, 1), :], ya_ref[8, pl.ds(x, 1), :])
        y_above = jnp.where(even_y, ya_ref[8, pl.ds(x, 1), :], yb_ref[8, pl.ds(x, 1), :])
        lower_y_rate = split(
            0.5 * (jnp.where(row == 0, y_below, pltpu.roll(speed_y, 1, 0)) + speed_y)
        )
        upper_y_rate = split(
            0.5
            * (
                speed_y
                + jnp.where(row == width_y - 1, y_above, pltpu.roll(speed_y, width_y - 1, 0))
            )
        )
        first = lane == 0
        last = lane == depth_z - 1
        rate = split(0.5 * (jnp.where(first, 0.0, pltpu.roll(speed_z, 1, 1)) + speed_z))
        lower_z_rate = (jnp.where(first, 0.0, rate[0]), rate[1])
        rate = split(
            0.5 * (speed_z + jnp.where(last, 0.0, pltpu.roll(speed_z, depth_z - 1, 1)))
        )
        upper_z_rate = (rate[0], jnp.where(last, 0.0, rate[1]))
        drift = (1.5 * speed_x, 1.5 * speed_y, 1.5 * speed_z)
        upper_x = []
        for field in range(2):
            state = [state_ref[field * 8 + corner, x] for corner in range(8)]
            result = list(state)

            def update(low, high, low_flux, high_flux, d):
                both = low_flux + high_flux
                flow = drift[d] * (state[low] + state[high])
                result[low] = result[low] + ((both + low_flux) - flow)
                result[high] = result[high] + (flow - (both + high_flux))

            for k in range(4):
                low, high = k, k + 4
                across = (
                    above_x(field * 4 + k)
                    if x == width_x - 1
                    else state_ref[field * 8 + k, x + 1]
                )
                flux = upper_x_rate[0] * state[high] + upper_x_rate[1] * across
                upper_x.append(flux)
                update(low, high, lower_x[field * 4 + k], flux, 0)
            for a in range(2):
                for c in range(2):
                    low = a * 4 + c
                    high = low + 2
                    k = field * 4 + a * 2 + c
                    ya = ya_ref[k, pl.ds(x, 1), :]
                    yb = yb_ref[k, pl.ds(x, 1), :]
                    left = jnp.where(
                        row == 0, jnp.where(even_y, yb, ya), pltpu.roll(state[high], 1, 0)
                    )
                    right = jnp.where(
                        row == width_y - 1,
                        jnp.where(even_y, ya, yb),
                        pltpu.roll(state[low], width_y - 1, 0),
                    )
                    update(
                        low,
                        high,
                        lower_y_rate[0] * left + lower_y_rate[1] * state[low],
                        upper_y_rate[0] * state[high] + upper_y_rate[1] * right,
                        1,
                    )
            for k in range(4):
                low, high = 2 * k, 2 * k + 1
                left = pltpu.roll(state[high], 1, 1)
                right = pltpu.roll(state[low], depth_z - 1, 1)
                update(
                    low,
                    high,
                    lower_z_rate[0] * left + lower_z_rate[1] * state[low],
                    upper_z_rate[0] * state[high] + upper_z_rate[1] * right,
                    2,
                )
            part = None
            for corner in range(8):
                out_ref[field * 8 + corner, x] = result[corner]
                part = result[corner] if part is None else part + result[corner]
            totals[field] = part if totals[field] is None else totals[field] + part
        lower_x = upper_x
    total_ref[...] = jnp.broadcast_to(folded(totals)[None], total_ref.shape)
    for copy in copies:
        copy.wait()
    half = lax.broadcasted_iota(jnp.int32, goal_ref.shape, 1) < depth_z // 2
    goal_ref[...] = jnp.where(half, targets_ref[0], targets_ref[1])
    place = lax.axis_index("py")
    rows = out_ref.reshape(16 * width_x * width_y, depth_z)
    owners = [owners_ref[0, entry, 0] for entry in range(entries)]
    for entry in range(entries):
        slot = jnp.int32(0)
        for earlier in range(entry):
            slot = slot + jnp.where(owners[earlier] == owners[entry], 1, 0)
        if count_py & (count_py - 1) == 0:
            hop = owners[entry] ^ place
        else:
            hop = lax.rem(owners[entry] - place + count_py, count_py)
        sending[hop * capacity + slot] = rows[
            pl.ds(blocks_ref[0, entry], 16, stride=width_x * width_y), :
        ]
    for hop in range(count_py):
        send_refs[hop][...] = sending[pl.ds(hop * capacity, capacity)]


def folded(totals):
    rows = [jnp.sum(total, axis=0, keepdims=True) for total in totals]
    depth = rows[0].shape[1]
    rows = [row + pltpu.roll(row, depth // 2, 1) for row in rows]
    half = lax.broadcasted_iota(jnp.int32, rows[0].shape, 1) < depth // 2
    return jnp.where(half, rows[0], rows[1])


def remap_call(state, relative, halos, blocks, owners, targets, device_count, count_py):
    sizes = state.shape[1:]
    width_x, width_y, depth_z = sizes
    entries = blocks.shape[1]
    capacity = max(2, 2 * entries // count_py)
    return pl.pallas_call(
        functools.partial(remap_kernel, sizes, count_py, entries, capacity),
        out_shape=(
            shape_of(16, *sizes),
            shape_of(device_count, 1, depth_z),
            shape_of(1, depth_z),
        )
        + (shape_of(capacity, 16, depth_z),) * count_py,
        in_specs=[in_vmem()] * 6 + [in_place()] * 3,
        out_specs=(in_vmem(),) * (3 + count_py),
        scratch_shapes=[
            pltpu.VMEM((count_py * capacity, 16, depth_z), jnp.float32),
            pltpu.SMEM(blocks.shape, jnp.int32),
            pltpu.SMEM(owners.shape, jnp.int32),
            pltpu.SMEM(targets.shape, jnp.float32),
            pltpu.SemaphoreType.DMA((3,)),
        ],
        compiler_params=kernel_options(),
        name="remap",
    )(state, relative, *halos, blocks, owners, targets)


def scale_kernel(total_nodes, state_ref, total_ref, goal_ref, fixed_ref, scale_ref):
    total = jnp.sum(total_ref[...], axis=0)
    half = lax.broadcasted_iota(jnp.int32, total.shape, 1) < total.shape[1] // 2
    sums = (
        jnp.sum(jnp.where(half, total, 0.0), axis=1, keepdims=True),
        jnp.sum(jnp.where(half, 0.0, total), axis=1, keepdims=True),
    )
    means = jnp.where(half, sums[0], sums[1]) / total_nodes
    scale = goal_ref[...] / means
    other = pltpu.roll(scale, scale.shape[1] // 2, 1)
    factors = (jnp.where(half, scale, other), jnp.where(half, other, scale))
    for field in range(2):
        scale_ref[pl.ds(field, 1), :] = factors[field]
        fixed_ref[pl.ds(field * 8, 8)] = state_ref[pl.ds(field * 8, 8)] * factors[field]


def scale_call(state, gathered, goal, total_nodes):
    return pl.pallas_call(
        functools.partial(scale_kernel, total_nodes),
        out_shape=(shape_of(*state.shape), shape_of(2, state.shape[-1])),
        in_specs=[in_vmem()] * 3,
        out_specs=(in_vmem(),) * 2,
        compiler_params=kernel_options(),
        name="scale",
    )(state, gathered, goal)


def settle_kernel(count_py, capacity, scale_ref, *refs):
    handed_ref = refs[count_py]
    place = lax.axis_index("py")
    for hop in range(count_py):
        start = giver_of(place, hop, count_py) * capacity
        for field in range(2):
            handed_ref[pl.ds(start, capacity), pl.ds(field * 8, 8), :] = (
                refs[hop][:, pl.ds(field * 8, 8), :] * scale_ref[pl.ds(field, 1), :]
            )


def settle_call(scale, chunks):
    count_py = len(chunks)
    capacity = chunks[0].shape[0]
    return pl.pallas_call(
        functools.partial(settle_kernel, count_py, capacity),
        out_shape=shape_of(count_py * capacity, *chunks[0].shape[1:]),
        in_specs=[in_vmem()] * (1 + count_py),
        out_specs=in_vmem(),
        compiler_params=kernel_options(),
        name="settle",
    )(scale, *chunks)


def hop_pairs(size, hop):
    if size & (size - 1) == 0:
        return [(i, i ^ hop) for i in range(size)]
    return [(i, (i + hop) % size) for i in range(size)]


def body(conserved, velocity, targets, handoff_blocks, handoff_owner):
    count_px = lax.axis_size("px")
    count_py = lax.axis_size("py")
    device_count = count_px * count_py
    total_nodes = 8.0 * math.prod(conserved.shape[4:]) * device_count
    state, relative, xa, xb, ya, yb = lagrange_call(conserved, velocity)
    halos = (
        lax.ppermute(xa, "px", paired(count_px, 0)),
        lax.ppermute(xb, "px", paired(count_px, 1)),
        lax.ppermute(ya, "py", paired(count_py, 0)),
        lax.ppermute(yb, "py", paired(count_py, 1)),
    )
    remapped, total, goal, *chunks = remap_call(
        state, relative, halos, handoff_blocks, handoff_owner, targets, device_count, count_py
    )
    received = [chunks[0]] + [
        lax.ppermute(chunks[hop], "py", hop_pairs(count_py, hop)) for hop in range(1, count_py)
    ]
    gathered = lax.all_to_all(total, ("px", "py"), 0, 0, tiled=True)
    fixed, scale = scale_call(remapped, gathered, goal, total_nodes)
    handed = settle_call(scale, received)
    return fixed.reshape(conserved.shape), handed[None]


def solution(mesh):
    return jax.shard_map(
        body,
        mesh=mesh,
        in_specs=(
            P(None, None, None, None, "px", "py", None),
            P(None, None, None, None, "px", "py", None),
            P(),
            P("px", "py"),
            P("px", "py", None),
        ),
        out_specs=(P(None, None, None, None, "px", "py", None), P("px", "py", None, None)),
        check_vma=False,
    )
```

```python
import functools
import math

import jax
import jax.numpy as jnp
from jax import lax
from jax.experimental import pallas as pl
from jax.experimental.pallas import tpu as pltpu
from jax.sharding import PartitionSpec as P

gamma_less = 0.4
force_step = 0.02
gauss_offset = 0.5 / math.sqrt(3.0)


def in_vmem():
    return pl.BlockSpec(memory_space=pltpu.VMEM)


def in_place():
    return pl.BlockSpec(memory_space=pltpu.HBM)


def shape_of(*shape):
    return jax.ShapeDtypeStruct(shape, jnp.float32)


def kernel_options():
    return pltpu.CompilerParams(vmem_limit_bytes=16 * 1024 * 1024)


def exchanges(counts, axis, first):
    pairs = []
    for i in range(counts[0]):
        for j in range(counts[1]):
            place = [i, j]
            partner = list(place)
            along_axis = place[axis] + 1 if (place[axis] - first) % 2 == 0 else place[axis] - 1
            if 0 <= along_axis < counts[axis]:
                partner[axis] = along_axis
            elif place[1 - axis] ^ 1 < counts[1 - axis]:
                partner[1 - axis] = place[1 - axis] ^ 1
            pairs.append((i * counts[1] + j, partner[0] * counts[1] + partner[1]))
    return pairs


def giver_of(index, hop, size):
    if size & (size - 1) == 0:
        return index ^ hop
    return lax.rem(index + size - hop, size)


def lifted(low, high, value):
    middle = 0.5 * (low + high)
    tilt = value * (low - high)
    return middle + tilt, middle - tilt


def along(values, direction, operation):
    stride = (4, 2, 1)[direction]
    out = [None] * 8
    for low in range(8):
        if not low & stride:
            out[low], out[low + stride] = operation(values[low], values[low + stride])
    return out


def quadratic_values(first, second, third):
    middle = (1.0 / 6.0) * (first + third) + (2.0 / 3.0) * second
    tilt = gauss_offset * (third - first)
    return middle - tilt, middle + tilt


def quadratic_slopes(first, second, third):
    rise = third - first
    bend = (4.0 * gauss_offset) * ((first + third) - 2.0 * second)
    return rise - bend, rise + bend


def lagrange_kernel(
    sizes,
    conserved_ref,
    velocity_ref,
    state_ref,
    relative_ref,
    xa_ref,
    xb_ref,
    ya_ref,
    yb_ref,
    motion_ref,
    state_sem,
    motion_sem,
):
    width_x, width_y, depth_z = sizes
    copies = []
    for x in range(width_x):
        copies.append(
            (
                pltpu.make_async_copy(
                    conserved_ref.at[:, x], state_ref.at[:, x], state_sem.at[x]
                ),
                pltpu.make_async_copy(
                    velocity_ref.at[:, x], motion_ref.at[:, x], motion_sem.at[x]
                ),
            )
        )
    for state_copy, motion_copy in copies:
        state_copy.start()
        motion_copy.start()
    lane = lax.broadcasted_iota(jnp.int32, (width_y, depth_z), 1)
    for x in range(width_x):
        copies[x][0].wait()
        copies[x][1].wait()
        divergence = [None] * 8
        for component in range(3):

            def node(a, b, c):
                return motion_ref[component * 27 + a * 9 + b * 3 + c, x]

            total = None
            stage = {}
            for a in range(3):
                for b in range(3):
                    line = [node(a, b, c) for c in range(3)]
                    part = (line[0] + line[1]) + line[2]
                    total = part if total is None else total + part
                    rule = quadratic_slopes if component == 2 else quadratic_values
                    stage[a, b, 0], stage[a, b, 1] = rule(*line)
            second = {}
            for a in range(3):
                for c in range(2):
                    rule = quadratic_slopes if component == 1 else quadratic_values
                    second[a, 0, c], second[a, 1, c] = rule(
                        stage[a, 0, c], stage[a, 1, c], stage[a, 2, c]
                    )
            for b in range(2):
                for c in range(2):
                    rule = quadratic_slopes if component == 0 else quadratic_values
                    pair = rule(second[0, b, c], second[1, b, c], second[2, b, c])
                    for a in range(2):
                        point = a * 4 + b * 2 + c
                        divergence[point] = (
                            pair[a] if component == 0 else divergence[point] + pair[a]
                        )
            mean = total * (1.0 / 27.0)
            before = jnp.where(lane == 0, 0.0, pltpu.roll(mean, 1, 1))
            after = jnp.where(lane == depth_z - 1, 0.0, pltpu.roll(mean, depth_z - 1, 1))
            relative_ref[component, x] = mean - 0.25 * ((before + 2.0 * mean) + after)
        energy = [state_ref[8 + corner, x] for corner in range(8)]
        work = energy
        for direction in range(3):
            work = along(work, direction, lambda p, q: lifted(p, q, gauss_offset))
        work = [(gamma_less * work[point]) * divergence[point] for point in range(8)]
        for direction in range(3):
            work = along(work, direction, lambda p, q: lifted(p, q, 3.0 * gauss_offset))
        for corner in range(8):
            state_ref[8 + corner, x] = energy[corner] - force_step * work[corner]
    odd_x = lax.rem(lax.axis_index("px"), 2)
    for out_ref, side in ((xa_ref, 1 - odd_x), (xb_ref, odd_x)):
        place = side * (width_x - 1)
        for field in range(2):
            for k in range(4):
                out_ref[field * 4 + k] = state_ref[field * 8 + side * 4 + k, place]
        out_ref[8] = relative_ref[0, place]
    odd_y = lax.rem(lax.axis_index("py"), 2)
    state_rows = state_ref.reshape(16 * width_x * width_y, depth_z)
    relative_rows = relative_ref.reshape(3 * width_x * width_y, depth_z)
    column = width_x * width_y
    for out_ref, side in ((ya_ref, 1 - odd_y), (yb_ref, odd_y)):
        place = side * (width_y - 1)
        for field in range(2):
            for a in range(2):
                for c in range(2):
                    start = (field * 8 + a * 4 + c) * column + side * 2 * column + place
                    out_ref[field * 4 + a * 2 + c] = state_rows[
                        pl.ds(start, width_x, stride=width_y), :
                    ]
        out_ref[8] = relative_rows[pl.ds(column + place, width_x, stride=width_y), :]


def lagrange_call(conserved, velocity):
    width_x, width_y, depth_z = conserved.shape[4:]
    sizes = (width_x, width_y, depth_z)
    return pl.pallas_call(
        functools.partial(lagrange_kernel, sizes),
        out_shape=(
            shape_of(16, *sizes),
            shape_of(3, *sizes),
            shape_of(9, width_y, depth_z),
            shape_of(9, width_y, depth_z),
            shape_of(9, width_x, depth_z),
            shape_of(9, width_x, depth_z),
        ),
        in_specs=[in_place()] * 2,
        out_specs=(in_vmem(),) * 6,
        scratch_shapes=[
            pltpu.VMEM((81,) + sizes, jnp.float32),
            pltpu.SemaphoreType.DMA((width_x,)),
            pltpu.SemaphoreType.DMA((width_x,)),
        ],
        compiler_params=kernel_options(),
        name="lagrange",
    )(
        pltpu.with_memory_space_constraint(conserved.reshape((16,) + sizes), pltpu.HBM),
        pltpu.with_memory_space_constraint(velocity.reshape((81,) + sizes), pltpu.HBM),
    )


def remap_kernel(
    sizes,
    count_py,
    entries,
    capacity,
    state_ref,
    relative_ref,
    xa_ref,
    xb_ref,
    ya_ref,
    yb_ref,
    blocks_hbm,
    owners_hbm,
    targets_hbm,
    *refs,
):
    width_x, width_y, depth_z = sizes
    out_ref, total_ref, goal_ref = refs[:3]
    send_refs = refs[3 : 3 + count_py]
    sending, blocks_ref, owners_ref, targets_ref, sems = refs[3 + count_py :]
    copies = [
        pltpu.make_async_copy(blocks_hbm, blocks_ref, sems.at[0]),
        pltpu.make_async_copy(owners_hbm, owners_ref, sems.at[1]),
        pltpu.make_async_copy(targets_hbm, targets_ref, sems.at[2]),
    ]
    for copy in copies:
        copy.start()
    lane = lax.broadcasted_iota(jnp.int32, (width_y, depth_z), 1)
    row = lax.broadcasted_iota(jnp.int32, (width_y, depth_z), 0)
    index_x = lax.axis_index("px")
    index_y = lax.axis_index("py")
    even_x = lax.rem(index_x, 2) == 0
    even_y = lax.rem(index_y, 2) == 0
    some_below_x, some_above_x = index_x > 0, index_x < lax.axis_size("px") - 1
    some_below_y, some_above_y = index_y > 0, index_y < count_py - 1

    def below_x(k):
        return jnp.where(some_below_x, jnp.where(even_x, xb_ref[k], xa_ref[k]), 0.0)

    def above_x(k):
        return jnp.where(some_above_x, jnp.where(even_x, xa_ref[k], xb_ref[k]), 0.0)

    def below_y(k, x):
        ya, yb = ya_ref[k, pl.ds(x, 1), :], yb_ref[k, pl.ds(x, 1), :]
        return jnp.where(some_below_y, jnp.where(even_y, yb, ya), 0.0)

    def above_y(k, x):
        ya, yb = ya_ref[k, pl.ds(x, 1), :], yb_ref[k, pl.ds(x, 1), :]
        return jnp.where(some_above_y, jnp.where(even_y, ya, yb), 0.0)

    def split(speed):
        return jnp.maximum(speed, 0.0), jnp.minimum(speed, 0.0)

    sending[...] = jnp.zeros(sending.shape, jnp.float32)
    totals = [None, None]
    speed = relative_ref[0, 0]
    coefficient = split(0.5 * (below_x(8) + speed))
    lower_x = [
        coefficient[0] * below_x(field * 4 + k) + coefficient[1] * state_ref[field * 8 + k, 0]
        for field in range(2)
        for k in range(4)
    ]
    for x in range(width_x):
        speed_x, speed_y, speed_z = (relative_ref[d, x] for d in range(3))
        beyond = above_x(8) if x == width_x - 1 else relative_ref[0, x + 1]
        upper_x_rate = split(0.5 * (speed_x + beyond))
        y_below, y_above = below_y(8, x), above_y(8, x)
        lower_y_rate = split(
            0.5 * (jnp.where(row == 0, y_below, pltpu.roll(speed_y, 1, 0)) + speed_y)
        )
        upper_y_rate = split(
            0.5
            * (
                speed_y
                + jnp.where(row == width_y - 1, y_above, pltpu.roll(speed_y, width_y - 1, 0))
            )
        )
        first = lane == 0
        last = lane == depth_z - 1
        rate = split(0.5 * (jnp.where(first, 0.0, pltpu.roll(speed_z, 1, 1)) + speed_z))
        lower_z_rate = (jnp.where(first, 0.0, rate[0]), rate[1])
        rate = split(
            0.5 * (speed_z + jnp.where(last, 0.0, pltpu.roll(speed_z, depth_z - 1, 1)))
        )
        upper_z_rate = (rate[0], jnp.where(last, 0.0, rate[1]))
        drift = (1.5 * speed_x, 1.5 * speed_y, 1.5 * speed_z)
        upper_x = []
        for field in range(2):
            state = [state_ref[field * 8 + corner, x] for corner in range(8)]
            result = list(state)

            def update(low, high, low_flux, high_flux, d):
                both = low_flux + high_flux
                flow = drift[d] * (state[low] + state[high])
                result[low] = result[low] + ((both + low_flux) - flow)
                result[high] = result[high] + (flow - (both + high_flux))

            for k in range(4):
                low, high = k, k + 4
                across = (
                    above_x(field * 4 + k)
                    if x == width_x - 1
                    else state_ref[field * 8 + k, x + 1]
                )
                flux = upper_x_rate[0] * state[high] + upper_x_rate[1] * across
                upper_x.append(flux)
                update(low, high, lower_x[field * 4 + k], flux, 0)
            for a in range(2):
                for c in range(2):
                    low = a * 4 + c
                    high = low + 2
                    k = field * 4 + a * 2 + c
                    left = jnp.where(row == 0, below_y(k, x), pltpu.roll(state[high], 1, 0))
                    right = jnp.where(
                        row == width_y - 1,
                        above_y(k, x),
                        pltpu.roll(state[low], width_y - 1, 0),
                    )
                    update(
                        low,
                        high,
                        lower_y_rate[0] * left + lower_y_rate[1] * state[low],
                        upper_y_rate[0] * state[high] + upper_y_rate[1] * right,
                        1,
                    )
            for k in range(4):
                low, high = 2 * k, 2 * k + 1
                left = pltpu.roll(state[high], 1, 1)
                right = pltpu.roll(state[low], depth_z - 1, 1)
                update(
                    low,
                    high,
                    lower_z_rate[0] * left + lower_z_rate[1] * state[low],
                    upper_z_rate[0] * state[high] + upper_z_rate[1] * right,
                    2,
                )
            part = None
            for corner in range(8):
                out_ref[field * 8 + corner, x] = result[corner]
                part = result[corner] if part is None else part + result[corner]
            totals[field] = part if totals[field] is None else totals[field] + part
        lower_x = upper_x
    total_ref[...] = jnp.broadcast_to(folded(totals)[None], total_ref.shape)
    for copy in copies:
        copy.wait()
    half = lax.broadcasted_iota(jnp.int32, goal_ref.shape, 1) < depth_z // 2
    goal_ref[...] = jnp.where(half, targets_ref[0], targets_ref[1])
    place = index_y
    rows = out_ref.reshape(16 * width_x * width_y, depth_z)
    owners = [owners_ref[0, entry, 0] for entry in range(entries)]
    for entry in range(entries):
        slot = jnp.int32(0)
        for earlier in range(entry):
            slot = slot + jnp.where(owners[earlier] == owners[entry], 1, 0)
        if count_py & (count_py - 1) == 0:
            hop = owners[entry] ^ place
        else:
            hop = lax.rem(owners[entry] - place + count_py, count_py)
        sending[hop * capacity + slot] = rows[
            pl.ds(blocks_ref[0, entry], 16, stride=width_x * width_y), :
        ]
    for hop in range(count_py):
        send_refs[hop][...] = sending[pl.ds(hop * capacity, capacity)]


def folded(totals):
    rows = [jnp.sum(total, axis=0, keepdims=True) for total in totals]
    depth = rows[0].shape[1]
    rows = [row + pltpu.roll(row, depth // 2, 1) for row in rows]
    half = lax.broadcasted_iota(jnp.int32, rows[0].shape, 1) < depth // 2
    return jnp.where(half, rows[0], rows[1])


def remap_call(state, relative, halos, blocks, owners, targets, device_count, count_py):
    sizes = state.shape[1:]
    width_x, width_y, depth_z = sizes
    entries = blocks.shape[1]
    capacity = max(2, 2 * entries // count_py)
    return pl.pallas_call(
        functools.partial(remap_kernel, sizes, count_py, entries, capacity),
        out_shape=(
            shape_of(16, *sizes),
            shape_of(device_count, 1, depth_z),
            shape_of(1, depth_z),
        )
        + (shape_of(capacity, 16, depth_z),) * count_py,
        in_specs=[in_vmem()] * 6 + [in_place()] * 3,
        out_specs=(in_vmem(),) * (3 + count_py),
        scratch_shapes=[
            pltpu.VMEM((count_py * capacity, 16, depth_z), jnp.float32),
            pltpu.SMEM(blocks.shape, jnp.int32),
            pltpu.SMEM(owners.shape, jnp.int32),
            pltpu.SMEM(targets.shape, jnp.float32),
            pltpu.SemaphoreType.DMA((3,)),
        ],
        compiler_params=kernel_options(),
        name="remap",
    )(state, relative, *halos, blocks, owners, targets)


def scale_kernel(total_nodes, state_ref, total_ref, goal_ref, fixed_ref, scale_ref):
    total = jnp.sum(total_ref[...], axis=0)
    half = lax.broadcasted_iota(jnp.int32, total.shape, 1) < total.shape[1] // 2
    sums = (
        jnp.sum(jnp.where(half, total, 0.0), axis=1, keepdims=True),
        jnp.sum(jnp.where(half, 0.0, total), axis=1, keepdims=True),
    )
    means = jnp.where(half, sums[0], sums[1]) / total_nodes
    scale = goal_ref[...] / means
    other = pltpu.roll(scale, scale.shape[1] // 2, 1)
    factors = (jnp.where(half, scale, other), jnp.where(half, other, scale))
    for field in range(2):
        scale_ref[pl.ds(field, 1), :] = factors[field]
        fixed_ref[pl.ds(field * 8, 8)] = state_ref[pl.ds(field * 8, 8)] * factors[field]


def scale_call(state, gathered, goal, total_nodes):
    return pl.pallas_call(
        functools.partial(scale_kernel, total_nodes),
        out_shape=(shape_of(*state.shape), shape_of(2, state.shape[-1])),
        in_specs=[in_vmem()] * 3,
        out_specs=(in_vmem(),) * 2,
        compiler_params=kernel_options(),
        name="scale",
    )(state, gathered, goal)


def settle_kernel(count_py, capacity, scale_ref, *refs):
    handed_ref = refs[count_py]
    place = lax.axis_index("py")
    for hop in range(count_py):
        start = giver_of(place, hop, count_py) * capacity
        for field in range(2):
            handed_ref[pl.ds(start, capacity), pl.ds(field * 8, 8), :] = (
                refs[hop][:, pl.ds(field * 8, 8), :] * scale_ref[pl.ds(field, 1), :]
            )


def settle_call(scale, chunks):
    count_py = len(chunks)
    capacity = chunks[0].shape[0]
    return pl.pallas_call(
        functools.partial(settle_kernel, count_py, capacity),
        out_shape=shape_of(count_py * capacity, *chunks[0].shape[1:]),
        in_specs=[in_vmem()] * (1 + count_py),
        out_specs=in_vmem(),
        compiler_params=kernel_options(),
        name="settle",
    )(scale, *chunks)


def hop_pairs(size, hop):
    if size & (size - 1) == 0:
        return [(i, i ^ hop) for i in range(size)]
    return [(i, (i + hop) % size) for i in range(size)]


def body(conserved, velocity, targets, handoff_blocks, handoff_owner):
    count_px = lax.axis_size("px")
    count_py = lax.axis_size("py")
    device_count = count_px * count_py
    total_nodes = 8.0 * math.prod(conserved.shape[4:]) * device_count
    state, relative, xa, xb, ya, yb = lagrange_call(conserved, velocity)
    counts = (count_px, count_py)
    halos = tuple(
        lax.ppermute(message, ("px", "py"), exchanges(counts, axis, first))
        for message, axis, first in ((xa, 0, 0), (xb, 0, 1), (ya, 1, 0), (yb, 1, 1))
    )
    remapped, total, goal, *chunks = remap_call(
        state, relative, halos, handoff_blocks, handoff_owner, targets, device_count, count_py
    )
    received = [chunks[0]] + [
        lax.ppermute(chunks[hop], "py", hop_pairs(count_py, hop)) for hop in range(1, count_py)
    ]
    gathered = lax.all_to_all(total, ("px", "py"), 0, 0, tiled=True)
    fixed, scale = scale_call(remapped, gathered, goal, total_nodes)
    handed = settle_call(scale, received)
    return fixed.reshape(conserved.shape), handed[None]


def solution(mesh):
    return jax.shard_map(
        body,
        mesh=mesh,
        in_specs=(
            P(None, None, None, None, "px", "py", None),
            P(None, None, None, None, "px", "py", None),
            P(),
            P("px", "py"),
            P("px", "py", None),
        ),
        out_specs=(P(None, None, None, None, "px", "py", None), P("px", "py", None, None)),
        check_vma=False,
    )
```

```python
import functools
import math

import jax
import jax.numpy as jnp
from jax import lax
from jax.experimental import pallas as pl
from jax.experimental.pallas import tpu as pltpu
from jax.sharding import PartitionSpec as P


gamma_less = 0.4
force_step = 0.02
gauss_offset = 0.5 / math.sqrt(3.0)


def in_vmem():
    return pl.BlockSpec(memory_space=pltpu.VMEM)


def in_place():
    return pl.BlockSpec(memory_space=pltpu.HBM)


def shape_of(*shape):
    return jax.ShapeDtypeStruct(shape, jnp.float32)


def kernel_options():
    return pltpu.CompilerParams(vmem_limit_bytes=16 * 1024 * 1024)


def exchanges(counts, axis, first):
    pairs = []
    for i in range(counts[0]):
        for j in range(counts[1]):
            place = [i, j]
            partner = list(place)
            along_axis = place[axis] + 1 if (place[axis] - first) % 2 == 0 else place[axis] - 1
            if 0 <= along_axis < counts[axis]:
                partner[axis] = along_axis
            elif place[1 - axis] ^ 1 < counts[1 - axis]:
                partner[1 - axis] = place[1 - axis] ^ 1
            pairs.append((i * counts[1] + j, partner[0] * counts[1] + partner[1]))
    return pairs


def giver_of(index, hop, size):
    if size & (size - 1) == 0:
        return index ^ hop
    return lax.rem(index + size - hop, size)


def lifted(low, high, value):
    middle = 0.5 * (low + high)
    tilt = value * (low - high)
    return middle + tilt, middle - tilt


def along(values, direction, operation):
    stride = (4, 2, 1)[direction]
    out = [None] * 8
    for low in range(8):
        if not low & stride:
            out[low], out[low + stride] = operation(values[low], values[low + stride])
    return out


def added(values):
    while len(values) > 1:
        values = [values[i] + values[i + 1] for i in range(0, len(values) - 1, 2)] + (
            [values[-1]] if len(values) % 2 else []
        )
    return values[0]


def quadratic_values(first, second, third):
    middle = (1.0 / 6.0) * (first + third) + (2.0 / 3.0) * second
    tilt = gauss_offset * (third - first)
    return middle - tilt, middle + tilt


def quadratic_slopes(first, second, third):
    rise = third - first
    bend = (4.0 * gauss_offset) * ((first + third) - 2.0 * second)
    return rise - bend, rise + bend


def lagrange_kernel(
    sizes,
    conserved_ref,
    velocity_ref,
    state_ref,
    relative_ref,
    xa_ref,
    xb_ref,
    ya_ref,
    yb_ref,
    total_hbm,
    motion_ref,
    total_ref,
    state_sem,
    motion_sem,
    total_sem,
):
    width_x, width_y, depth_z = sizes
    copies = []
    for x in range(width_x):
        copies.append(
            (
                pltpu.make_async_copy(
                    conserved_ref.at[:, x], state_ref.at[:, x], state_sem.at[x]
                ),
                pltpu.make_async_copy(
                    velocity_ref.at[:, x], motion_ref.at[:, x], motion_sem.at[x]
                ),
            )
        )
    for state_copy, motion_copy in copies:
        state_copy.start()
        motion_copy.start()
    lane = lax.broadcasted_iota(jnp.int32, (width_y, depth_z), 1)
    row = lax.broadcasted_iota(jnp.int32, (width_y, depth_z), 0)
    index_x, index_y = lax.axis_index("px"), lax.axis_index("py")
    first_y = jnp.logical_and(row == 0, index_y == 0)
    last_y = jnp.logical_and(row == width_y - 1, index_y == lax.axis_size("py") - 1)
    totals = [None, None]
    for x in range(width_x):
        copies[x][0].wait()
        copies[x][1].wait()
        divergence = [None] * 8
        motion = []
        for component in range(3):

            def node(a, b, c):
                return motion_ref[component * 27 + a * 9 + b * 3 + c, x]

            total = None
            stage = {}
            for a in range(3):
                for b in range(3):
                    line = [node(a, b, c) for c in range(3)]
                    part = (line[0] + line[1]) + line[2]
                    total = part if total is None else total + part
                    rule = quadratic_slopes if component == 2 else quadratic_values
                    stage[a, b, 0], stage[a, b, 1] = rule(*line)
            second = {}
            for a in range(3):
                for c in range(2):
                    rule = quadratic_slopes if component == 1 else quadratic_values
                    second[a, 0, c], second[a, 1, c] = rule(
                        stage[a, 0, c], stage[a, 1, c], stage[a, 2, c]
                    )
            for b in range(2):
                for c in range(2):
                    rule = quadratic_slopes if component == 0 else quadratic_values
                    pair = rule(second[0, b, c], second[1, b, c], second[2, b, c])
                    for a in range(2):
                        point = a * 4 + b * 2 + c
                        divergence[point] = (
                            pair[a] if component == 0 else divergence[point] + pair[a]
                        )
            mean = total * (1.0 / 27.0)
            before = jnp.where(lane == 0, 0.0, pltpu.roll(mean, 1, 1))
            after = jnp.where(lane == depth_z - 1, 0.0, pltpu.roll(mean, depth_z - 1, 1))
            motion.append(mean - 0.25 * ((before + 2.0 * mean) + after))
            relative_ref[component, x] = motion[component]
        energy = [state_ref[8 + corner, x] for corner in range(8)]
        work = energy
        for direction in range(3):
            work = along(work, direction, lambda p, q: lifted(p, q, gauss_offset))
        work = [(gamma_less * work[point]) * divergence[point] for point in range(8)]
        for direction in range(3):
            work = along(work, direction, lambda p, q: lifted(p, q, 3.0 * gauss_offset))
        energy = [energy[corner] - force_step * work[corner] for corner in range(8)]
        for corner in range(8):
            state_ref[8 + corner, x] = energy[corner]
        half_motion = [0.5 * speed for speed in motion]
        entering = [
            jnp.where(index_x == 0, jnp.minimum(half_motion[0], 0.0), 0.0) if x == 0 else None,
            jnp.where(first_y, jnp.minimum(half_motion[1], 0.0), 0.0),
            jnp.where(lane == 0, jnp.minimum(half_motion[2], 0.0), 0.0),
        ]
        leaving = [
            jnp.where(index_x == lax.axis_size("px") - 1, jnp.maximum(half_motion[0], 0.0), 0.0)
            if x == width_x - 1
            else None,
            jnp.where(last_y, jnp.maximum(half_motion[1], 0.0), 0.0),
            jnp.where(lane == depth_z - 1, jnp.maximum(half_motion[2], 0.0), 0.0),
        ]
        for field in range(2):
            values = energy if field else [state_ref[corner, x] for corner in range(8)]
            part = None
            for direction in range(3):
                stride = (4, 2, 1)[direction]
                low = added([values[k] for k in range(8) if not k & stride])
                high = added([values[k] for k in range(8) if k & stride])
                if part is None:
                    part = low + high
                if entering[direction] is not None:
                    part = part + entering[direction] * low
                if leaving[direction] is not None:
                    part = part - leaving[direction] * high
            totals[field] = part if totals[field] is None else totals[field] + part
    total_ref[...] = jnp.broadcast_to(folded(totals)[None], total_ref.shape)
    total_copy = pltpu.make_async_copy(total_ref, total_hbm, total_sem)
    total_copy.start()
    odd_x = lax.rem(index_x, 2)
    for out_ref, side in ((xa_ref, 1 - odd_x), (xb_ref, odd_x)):
        place = side * (width_x - 1)
        for field in range(2):
            for k in range(4):
                out_ref[field * 4 + k] = state_ref[field * 8 + side * 4 + k, place]
        out_ref[8] = relative_ref[0, place]
    odd_y = lax.rem(index_y, 2)
    state_rows = state_ref.reshape(16 * width_x * width_y, depth_z)
    relative_rows = relative_ref.reshape(3 * width_x * width_y, depth_z)
    column = width_x * width_y
    for out_ref, side in ((ya_ref, 1 - odd_y), (yb_ref, odd_y)):
        place = side * (width_y - 1)
        for field in range(2):
            for a in range(2):
                for c in range(2):
                    start = (field * 8 + a * 4 + c) * column + side * 2 * column + place
                    out_ref[field * 4 + a * 2 + c] = state_rows[
                        pl.ds(start, width_x, stride=width_y), :
                    ]
        out_ref[8] = relative_rows[pl.ds(column + place, width_x, stride=width_y), :]
    total_copy.wait()


def lagrange_call(conserved, velocity, device_count):
    width_x, width_y, depth_z = conserved.shape[4:]
    sizes = (width_x, width_y, depth_z)
    return pl.pallas_call(
        functools.partial(lagrange_kernel, sizes),
        out_shape=(
            shape_of(16, *sizes),
            shape_of(3, *sizes),
            shape_of(9, width_y, depth_z),
            shape_of(9, width_y, depth_z),
            shape_of(9, width_x, depth_z),
            shape_of(9, width_x, depth_z),
            shape_of(device_count, 1, depth_z),
        ),
        in_specs=[in_place()] * 2,
        out_specs=(in_vmem(),) * 6 + (in_place(),),
        scratch_shapes=[
            pltpu.VMEM((81,) + sizes, jnp.float32),
            pltpu.VMEM((device_count, 1, depth_z), jnp.float32),
            pltpu.SemaphoreType.DMA((width_x,)),
            pltpu.SemaphoreType.DMA((width_x,)),
            pltpu.SemaphoreType.DMA,
        ],
        compiler_params=kernel_options(),
        name="lagrange",
    )(
        pltpu.with_memory_space_constraint(conserved.reshape((16,) + sizes), pltpu.HBM),
        pltpu.with_memory_space_constraint(velocity.reshape((81,) + sizes), pltpu.HBM),
    )


def remap_kernel(
    sizes,
    count_py,
    entries,
    capacity,
    state_ref,
    relative_ref,
    xa_ref,
    xb_ref,
    ya_ref,
    yb_ref,
    blocks_hbm,
    owners_hbm,
    targets_hbm,
    *refs,
):
    width_x, width_y, depth_z = sizes
    out_ref, goal_ref = refs[:2]
    send_refs = refs[2 : 2 + count_py]
    sending, blocks_ref, owners_ref, targets_ref, sems = refs[2 + count_py :]
    copies = [
        pltpu.make_async_copy(blocks_hbm, blocks_ref, sems.at[0]),
        pltpu.make_async_copy(owners_hbm, owners_ref, sems.at[1]),
        pltpu.make_async_copy(targets_hbm, targets_ref, sems.at[2]),
    ]
    for copy in copies:
        copy.start()
    lane = lax.broadcasted_iota(jnp.int32, (width_y, depth_z), 1)
    row = lax.broadcasted_iota(jnp.int32, (width_y, depth_z), 0)
    index_x = lax.axis_index("px")
    index_y = lax.axis_index("py")
    even_x = lax.rem(index_x, 2) == 0
    even_y = lax.rem(index_y, 2) == 0
    some_below_x, some_above_x = index_x > 0, index_x < lax.axis_size("px") - 1
    some_below_y, some_above_y = index_y > 0, index_y < count_py - 1

    def below_x(k):
        return jnp.where(some_below_x, jnp.where(even_x, xb_ref[k], xa_ref[k]), 0.0)

    def above_x(k):
        return jnp.where(some_above_x, jnp.where(even_x, xa_ref[k], xb_ref[k]), 0.0)

    def below_y(k, x):
        ya, yb = ya_ref[k, pl.ds(x, 1), :], yb_ref[k, pl.ds(x, 1), :]
        return jnp.where(some_below_y, jnp.where(even_y, yb, ya), 0.0)

    def above_y(k, x):
        ya, yb = ya_ref[k, pl.ds(x, 1), :], yb_ref[k, pl.ds(x, 1), :]
        return jnp.where(some_above_y, jnp.where(even_y, ya, yb), 0.0)

    def split(speed):
        return jnp.maximum(speed, 0.0), jnp.minimum(speed, 0.0)

    sending[...] = jnp.zeros(sending.shape, jnp.float32)
    speed = relative_ref[0, 0]
    coefficient = split(0.5 * (below_x(8) + speed))
    lower_x = [
        coefficient[0] * below_x(field * 4 + k) + coefficient[1] * state_ref[field * 8 + k, 0]
        for field in range(2)
        for k in range(4)
    ]
    for x in range(width_x):
        speed_x, speed_y, speed_z = (relative_ref[d, x] for d in range(3))
        beyond = above_x(8) if x == width_x - 1 else relative_ref[0, x + 1]
        upper_x_rate = split(0.5 * (speed_x + beyond))
        y_below, y_above = below_y(8, x), above_y(8, x)
        lower_y_rate = split(
            0.5 * (jnp.where(row == 0, y_below, pltpu.roll(speed_y, 1, 0)) + speed_y)
        )
        upper_y_rate = split(
            0.5
            * (
                speed_y
                + jnp.where(row == width_y - 1, y_above, pltpu.roll(speed_y, width_y - 1, 0))
            )
        )
        first = lane == 0
        last = lane == depth_z - 1
        rate = split(0.5 * (jnp.where(first, 0.0, pltpu.roll(speed_z, 1, 1)) + speed_z))
        lower_z_rate = (jnp.where(first, 0.0, rate[0]), rate[1])
        rate = split(
            0.5 * (speed_z + jnp.where(last, 0.0, pltpu.roll(speed_z, depth_z - 1, 1)))
        )
        upper_z_rate = (rate[0], jnp.where(last, 0.0, rate[1]))
        drift = (1.5 * speed_x, 1.5 * speed_y, 1.5 * speed_z)
        upper_x = []
        for field in range(2):
            state = [state_ref[field * 8 + corner, x] for corner in range(8)]
            result = list(state)

            def update(low, high, low_flux, high_flux, d):
                both = low_flux + high_flux
                flow = drift[d] * (state[low] + state[high])
                result[low] = result[low] + ((both + low_flux) - flow)
                result[high] = result[high] + (flow - (both + high_flux))

            for k in range(4):
                low, high = k, k + 4
                across = (
                    above_x(field * 4 + k)
                    if x == width_x - 1
                    else state_ref[field * 8 + k, x + 1]
                )
                flux = upper_x_rate[0] * state[high] + upper_x_rate[1] * across
                upper_x.append(flux)
                update(low, high, lower_x[field * 4 + k], flux, 0)
            for a in range(2):
                for c in range(2):
                    low = a * 4 + c
                    high = low + 2
                    k = field * 4 + a * 2 + c
                    left = jnp.where(row == 0, below_y(k, x), pltpu.roll(state[high], 1, 0))
                    right = jnp.where(
                        row == width_y - 1,
                        above_y(k, x),
                        pltpu.roll(state[low], width_y - 1, 0),
                    )
                    update(
                        low,
                        high,
                        lower_y_rate[0] * left + lower_y_rate[1] * state[low],
                        upper_y_rate[0] * state[high] + upper_y_rate[1] * right,
                        1,
                    )
            for k in range(4):
                low, high = 2 * k, 2 * k + 1
                left = pltpu.roll(state[high], 1, 1)
                right = pltpu.roll(state[low], depth_z - 1, 1)
                update(
                    low,
                    high,
                    lower_z_rate[0] * left + lower_z_rate[1] * state[low],
                    upper_z_rate[0] * state[high] + upper_z_rate[1] * right,
                    2,
                )
            for corner in range(8):
                out_ref[field * 8 + corner, x] = result[corner]
        lower_x = upper_x
    for copy in copies:
        copy.wait()
    half = lax.broadcasted_iota(jnp.int32, goal_ref.shape, 1) < depth_z // 2
    goal_ref[...] = jnp.where(half, targets_ref[0], targets_ref[1])
    place = index_y
    rows = out_ref.reshape(16 * width_x * width_y, depth_z)
    owners = [owners_ref[0, entry] for entry in range(entries)]
    for entry in range(entries):
        slot = jnp.int32(0)
        for earlier in range(entry):
            slot = slot + jnp.where(owners[earlier] == owners[entry], 1, 0)
        if count_py & (count_py - 1) == 0:
            hop = owners[entry] ^ place
        else:
            hop = lax.rem(owners[entry] - place + count_py, count_py)
        sending[hop * capacity + slot] = rows[
            pl.ds(blocks_ref[0, entry], 16, stride=width_x * width_y), :
        ]
    for hop in range(count_py):
        send_refs[hop][...] = sending[pl.ds(hop * capacity, capacity)]


def folded(totals):
    rows = [jnp.sum(total, axis=0, keepdims=True) for total in totals]
    depth = rows[0].shape[1]
    rows = [row + pltpu.roll(row, depth // 2, 1) for row in rows]
    half = lax.broadcasted_iota(jnp.int32, rows[0].shape, 1) < depth // 2
    return jnp.where(half, rows[0], rows[1])


def remap_call(state, relative, halos, blocks, owners, targets, count_py):
    sizes = state.shape[1:]
    _, _, depth_z = sizes
    entries = blocks.shape[1]
    capacity = max(2, 2 * entries // count_py)
    return pl.pallas_call(
        functools.partial(remap_kernel, sizes, count_py, entries, capacity),
        out_shape=(shape_of(16, *sizes), shape_of(1, depth_z))
        + (shape_of(capacity, 16, depth_z),) * count_py,
        in_specs=[in_vmem()] * 6 + [in_place()] * 3,
        out_specs=(in_vmem(),) * (2 + count_py),
        scratch_shapes=[
            pltpu.VMEM((count_py * capacity, 16, depth_z), jnp.float32),
            pltpu.SMEM(blocks.shape, jnp.int32),
            pltpu.SMEM(owners.shape, jnp.int32),
            pltpu.SMEM(targets.shape, jnp.float32),
            pltpu.SemaphoreType.DMA((3,)),
        ],
        compiler_params=kernel_options(),
        name="remap",
    )(state, relative, *halos, blocks, owners, targets)


def finish_kernel(total_nodes, count_py, capacity, state_ref, total_ref, goal_ref, *refs):
    chunk_refs = refs[:count_py]
    fixed_hbm, handed_hbm, fixed_ref, handed_ref, sems = refs[count_py:]
    total = jnp.sum(total_ref[...], axis=0)
    half = lax.broadcasted_iota(jnp.int32, total.shape, 1) < total.shape[1] // 2
    sums = (
        jnp.sum(jnp.where(half, total, 0.0), axis=1, keepdims=True),
        jnp.sum(jnp.where(half, 0.0, total), axis=1, keepdims=True),
    )
    means = jnp.where(half, sums[0], sums[1]) / total_nodes
    scale = goal_ref[...] / means
    other = pltpu.roll(scale, scale.shape[1] // 2, 1)
    factors = (jnp.where(half, scale, other), jnp.where(half, other, scale))
    copies = []
    for field in range(2):
        part = pl.ds(field * 8, 8)
        fixed_ref[part] = state_ref[part] * factors[field]
        copies.append(pltpu.make_async_copy(fixed_ref.at[part], fixed_hbm.at[part], sems.at[field]))
        copies[-1].start()
    place = lax.axis_index("py")
    for hop in range(count_py):
        start = giver_of(place, hop, count_py) * capacity
        for field in range(2):
            part = pl.ds(field * 8, 8)
            handed_ref[pl.ds(start, capacity), part, :] = (
                chunk_refs[hop][:, part, :] * factors[field]
            )
    copies.append(pltpu.make_async_copy(handed_ref, handed_hbm, sems.at[2]))
    copies[-1].start()
    for copy in copies:
        copy.wait()


def finish_call(state, gathered, goal, chunks, total_nodes):
    count_py = len(chunks)
    capacity = chunks[0].shape[0]
    handed = (count_py * capacity,) + chunks[0].shape[1:]
    return pl.pallas_call(
        functools.partial(finish_kernel, total_nodes, count_py, capacity),
        out_shape=(shape_of(*state.shape), shape_of(*handed)),
        in_specs=[in_vmem()] * (3 + count_py),
        out_specs=(in_place(),) * 2,
        scratch_shapes=[
            pltpu.VMEM(state.shape, jnp.float32),
            pltpu.VMEM(handed, jnp.float32),
            pltpu.SemaphoreType.DMA((3,)),
        ],
        compiler_params=kernel_options(),
        name="finish",
    )(state, gathered, goal, *chunks)


def hop_pairs(size, hop):
    if size & (size - 1) == 0:
        return [(i, i ^ hop) for i in range(size)]
    return [(i, (i + hop) % size) for i in range(size)]


def step(conserved, velocity, targets, handoff_blocks, handoff_owner):
    count_px = lax.axis_size("px")
    count_py = lax.axis_size("py")
    device_count = count_px * count_py
    total_nodes = 8.0 * math.prod(conserved.shape[4:]) * device_count
    state, relative, xa, xb, ya, yb, total = lagrange_call(conserved, velocity, device_count)
    counts = (count_px, count_py)
    halos = []
    for message, axis, first in ((xa, 0, 0), (xb, 0, 1), (ya, 1, 0), (yb, 1, 1)):
        halos.append(lax.ppermute(message, ("px", "py"), exchanges(counts, axis, first)))
    gathered = lax.all_to_all(total, ("px", "py"), 0, 0, tiled=True)
    remapped, goal, *chunks = remap_call(
        state,
        relative,
        halos,
        handoff_blocks,
        handoff_owner.reshape(handoff_blocks.shape),
        targets,
        count_py,
    )
    received = [chunks[0]]
    for hop in range(1, count_py):
        received.append(lax.ppermute(chunks[hop], "py", hop_pairs(count_py, hop)))
    fixed, handed = finish_call(remapped, gathered, goal, received, total_nodes)
    return fixed.reshape(conserved.shape), handed[None]


def solution(mesh):
    return jax.shard_map(
        step,
        mesh=mesh,
        in_specs=(
            P(None, None, None, None, "px", "py", None),
            P(None, None, None, None, "px", "py", None),
            P(),
            P("px", "py"),
            P("px", "py", None),
        ),
        out_specs=(P(None, None, None, None, "px", "py", None), P("px", "py", None, None)),
        check_vma=False,
    )
```

```python
import functools
import math

import jax
import jax.numpy as jnp
from jax import lax
from jax.experimental import pallas as pl
from jax.experimental.pallas import tpu as pltpu
from jax.sharding import PartitionSpec as P


gamma_less = 0.4
force_step = 0.02
gauss_offset = 0.5 / math.sqrt(3.0)


def in_vmem():
    return pl.BlockSpec(memory_space=pltpu.VMEM)


def in_place():
    return pl.BlockSpec(memory_space=pltpu.HBM)


def shape_of(*shape):
    return jax.ShapeDtypeStruct(shape, jnp.float32)


def kernel_options():
    return pltpu.CompilerParams(vmem_limit_bytes=16 * 1024 * 1024)


def exchanges(counts, axis, first):
    pairs = []
    for i in range(counts[0]):
        for j in range(counts[1]):
            place = [i, j]
            partner = list(place)
            along_axis = place[axis] + 1 if (place[axis] - first) % 2 == 0 else place[axis] - 1
            if 0 <= along_axis < counts[axis]:
                partner[axis] = along_axis
            elif place[1 - axis] ^ 1 < counts[1 - axis]:
                partner[1 - axis] = place[1 - axis] ^ 1
            pairs.append((i * counts[1] + j, partner[0] * counts[1] + partner[1]))
    return pairs


def giver_of(index, hop, size):
    if size & (size - 1) == 0:
        return index ^ hop
    return lax.rem(index + size - hop, size)


def lifted(low, high, value):
    middle = 0.5 * (low + high)
    tilt = value * (low - high)
    return middle + tilt, middle - tilt


def along(values, direction, operation):
    stride = (4, 2, 1)[direction]
    out = [None] * 8
    for low in range(8):
        if not low & stride:
            out[low], out[low + stride] = operation(values[low], values[low + stride])
    return out


def added(values):
    while len(values) > 1:
        values = [values[i] + values[i + 1] for i in range(0, len(values) - 1, 2)] + (
            [values[-1]] if len(values) % 2 else []
        )
    return values[0]


def quadratic_values(first, second, third):
    middle = (1.0 / 6.0) * (first + third) + (2.0 / 3.0) * second
    tilt = gauss_offset * (third - first)
    return middle - tilt, middle + tilt


def quadratic_slopes(first, second, third):
    rise = third - first
    bend = (4.0 * gauss_offset) * ((first + third) - 2.0 * second)
    return rise - bend, rise + bend


def lagrange_kernel(
    sizes,
    conserved_ref,
    velocity_ref,
    state_ref,
    relative_ref,
    xa_ref,
    xb_ref,
    ya_ref,
    yb_ref,
    total_hbm,
    motion_ref,
    total_ref,
    state_sem,
    motion_sem,
    total_sem,
):
    width_x, width_y, depth_z = sizes
    copies = []
    for x in range(width_x):
        copies.append(
            (
                pltpu.make_async_copy(
                    conserved_ref.at[:, x], state_ref.at[:, x], state_sem.at[x]
                ),
                pltpu.make_async_copy(
                    velocity_ref.at[:, x], motion_ref.at[:, x], motion_sem.at[x]
                ),
            )
        )
    for state_copy, motion_copy in copies:
        state_copy.start()
        motion_copy.start()
    lane = lax.broadcasted_iota(jnp.int32, (width_y, depth_z), 1)
    row = lax.broadcasted_iota(jnp.int32, (width_y, depth_z), 0)
    index_x, index_y = lax.axis_index("px"), lax.axis_index("py")
    first_y = jnp.logical_and(row == 0, index_y == 0)
    last_y = jnp.logical_and(row == width_y - 1, index_y == lax.axis_size("py") - 1)
    totals = [None, None]
    for x in range(width_x):
        copies[x][0].wait()
        copies[x][1].wait()
        divergence = [None] * 8
        motion = []
        for component in range(3):

            def node(a, b, c):
                return motion_ref[component * 27 + a * 9 + b * 3 + c, x]

            total = None
            stage = {}
            for a in range(3):
                for b in range(3):
                    line = [node(a, b, c) for c in range(3)]
                    part = (line[0] + line[1]) + line[2]
                    total = part if total is None else total + part
                    rule = quadratic_slopes if component == 2 else quadratic_values
                    stage[a, b, 0], stage[a, b, 1] = rule(*line)
            second = {}
            for a in range(3):
                for c in range(2):
                    rule = quadratic_slopes if component == 1 else quadratic_values
                    second[a, 0, c], second[a, 1, c] = rule(
                        stage[a, 0, c], stage[a, 1, c], stage[a, 2, c]
                    )
            for b in range(2):
                for c in range(2):
                    rule = quadratic_slopes if component == 0 else quadratic_values
                    pair = rule(second[0, b, c], second[1, b, c], second[2, b, c])
                    for a in range(2):
                        point = a * 4 + b * 2 + c
                        divergence[point] = (
                            pair[a] if component == 0 else divergence[point] + pair[a]
                        )
            mean = total * (1.0 / 27.0)
            before = jnp.where(lane == 0, 0.0, pltpu.roll(mean, 1, 1))
            after = jnp.where(lane == depth_z - 1, 0.0, pltpu.roll(mean, depth_z - 1, 1))
            motion.append(mean - 0.25 * ((before + 2.0 * mean) + after))
            relative_ref[component, x] = motion[component]
        energy = [state_ref[8 + corner, x] for corner in range(8)]
        work = energy
        for direction in range(3):
            work = along(work, direction, lambda p, q: lifted(p, q, gauss_offset))
        work = [(gamma_less * work[point]) * divergence[point] for point in range(8)]
        for direction in range(3):
            work = along(work, direction, lambda p, q: lifted(p, q, 3.0 * gauss_offset))
        energy = [energy[corner] - force_step * work[corner] for corner in range(8)]
        for corner in range(8):
            state_ref[8 + corner, x] = energy[corner]
        half_motion = [0.5 * speed for speed in motion]
        entering = [
            jnp.where(index_x == 0, jnp.minimum(half_motion[0], 0.0), 0.0) if x == 0 else None,
            jnp.where(first_y, jnp.minimum(half_motion[1], 0.0), 0.0),
            jnp.where(lane == 0, jnp.minimum(half_motion[2], 0.0), 0.0),
        ]
        leaving = [
            jnp.where(index_x == lax.axis_size("px") - 1, jnp.maximum(half_motion[0], 0.0), 0.0)
            if x == width_x - 1
            else None,
            jnp.where(last_y, jnp.maximum(half_motion[1], 0.0), 0.0),
            jnp.where(lane == depth_z - 1, jnp.maximum(half_motion[2], 0.0), 0.0),
        ]
        for field in range(2):
            values = energy if field else [state_ref[corner, x] for corner in range(8)]
            part = None
            for direction in range(3):
                stride = (4, 2, 1)[direction]
                low = added([values[k] for k in range(8) if not k & stride])
                high = added([values[k] for k in range(8) if k & stride])
                if part is None:
                    part = low + high
                if entering[direction] is not None:
                    part = part + entering[direction] * low
                if leaving[direction] is not None:
                    part = part - leaving[direction] * high
            totals[field] = part if totals[field] is None else totals[field] + part
    total_ref[...] = jnp.broadcast_to(folded(totals)[None], total_ref.shape)
    total_copy = pltpu.make_async_copy(total_ref, total_hbm, total_sem)
    total_copy.start()
    odd_x = lax.rem(index_x, 2)
    for out_ref, side in ((xa_ref, 1 - odd_x), (xb_ref, odd_x)):
        place = side * (width_x - 1)
        for field in range(2):
            for k in range(4):
                out_ref[field * 4 + k] = state_ref[field * 8 + side * 4 + k, place]
        out_ref[8] = relative_ref[0, place]
    odd_y = lax.rem(index_y, 2)
    state_rows = state_ref.reshape(16 * width_x * width_y, depth_z)
    relative_rows = relative_ref.reshape(3 * width_x * width_y, depth_z)
    column = width_x * width_y
    for out_ref, side in ((ya_ref, 1 - odd_y), (yb_ref, odd_y)):
        place = side * (width_y - 1)
        for field in range(2):
            for a in range(2):
                for c in range(2):
                    start = (field * 8 + a * 4 + c) * column + side * 2 * column + place
                    out_ref[field * 4 + a * 2 + c] = state_rows[
                        pl.ds(start, width_x, stride=width_y), :
                    ]
        out_ref[8] = relative_rows[pl.ds(column + place, width_x, stride=width_y), :]
    total_copy.wait()


def lagrange_call(conserved, velocity, device_count):
    width_x, width_y, depth_z = conserved.shape[4:]
    sizes = (width_x, width_y, depth_z)
    return pl.pallas_call(
        functools.partial(lagrange_kernel, sizes),
        out_shape=(
            shape_of(16, *sizes),
            shape_of(3, *sizes),
            shape_of(9, width_y, depth_z),
            shape_of(9, width_y, depth_z),
            shape_of(9, width_x, depth_z),
            shape_of(9, width_x, depth_z),
            shape_of(device_count, 1, depth_z),
        ),
        in_specs=[in_place()] * 2,
        out_specs=(in_vmem(),) * 6 + (in_place(),),
        scratch_shapes=[
            pltpu.VMEM((81,) + sizes, jnp.float32),
            pltpu.VMEM((device_count, 1, depth_z), jnp.float32),
            pltpu.SemaphoreType.DMA((width_x,)),
            pltpu.SemaphoreType.DMA((width_x,)),
            pltpu.SemaphoreType.DMA,
        ],
        compiler_params=kernel_options(),
        name="lagrange",
    )(
        pltpu.with_memory_space_constraint(conserved.reshape((16,) + sizes), pltpu.HBM),
        pltpu.with_memory_space_constraint(velocity.reshape((81,) + sizes), pltpu.HBM),
    )


def remap_kernel(
    sizes,
    count_py,
    entries,
    capacity,
    state_ref,
    relative_ref,
    xa_ref,
    xb_ref,
    ya_ref,
    yb_ref,
    blocks_ref,
    owners_ref,
    targets_ref,
    *refs,
):
    width_x, width_y, depth_z = sizes
    out_ref, goal_ref = refs[:2]
    send_refs = refs[2 : 2 + count_py]
    (sending,) = refs[2 + count_py :]
    lane = lax.broadcasted_iota(jnp.int32, (width_y, depth_z), 1)
    row = lax.broadcasted_iota(jnp.int32, (width_y, depth_z), 0)
    index_x = lax.axis_index("px")
    index_y = lax.axis_index("py")
    even_x = lax.rem(index_x, 2) == 0
    even_y = lax.rem(index_y, 2) == 0
    some_below_x, some_above_x = index_x > 0, index_x < lax.axis_size("px") - 1
    some_below_y, some_above_y = index_y > 0, index_y < count_py - 1

    def below_x(k):
        return jnp.where(some_below_x, jnp.where(even_x, xb_ref[k], xa_ref[k]), 0.0)

    def above_x(k):
        return jnp.where(some_above_x, jnp.where(even_x, xa_ref[k], xb_ref[k]), 0.0)

    def below_y(k, x):
        ya, yb = ya_ref[k, pl.ds(x, 1), :], yb_ref[k, pl.ds(x, 1), :]
        return jnp.where(some_below_y, jnp.where(even_y, yb, ya), 0.0)

    def above_y(k, x):
        ya, yb = ya_ref[k, pl.ds(x, 1), :], yb_ref[k, pl.ds(x, 1), :]
        return jnp.where(some_above_y, jnp.where(even_y, ya, yb), 0.0)

    def split(speed):
        return jnp.maximum(speed, 0.0), jnp.minimum(speed, 0.0)

    sending[...] = jnp.zeros(sending.shape, jnp.float32)
    speed = relative_ref[0, 0]
    coefficient = split(0.5 * (below_x(8) + speed))
    lower_x = [
        coefficient[0] * below_x(field * 4 + k) + coefficient[1] * state_ref[field * 8 + k, 0]
        for field in range(2)
        for k in range(4)
    ]
    for x in range(width_x):
        speed_x, speed_y, speed_z = (relative_ref[d, x] for d in range(3))
        beyond = above_x(8) if x == width_x - 1 else relative_ref[0, x + 1]
        upper_x_rate = split(0.5 * (speed_x + beyond))
        y_below, y_above = below_y(8, x), above_y(8, x)
        lower_y_rate = split(
            0.5 * (jnp.where(row == 0, y_below, pltpu.roll(speed_y, 1, 0)) + speed_y)
        )
        upper_y_rate = split(
            0.5
            * (
                speed_y
                + jnp.where(row == width_y - 1, y_above, pltpu.roll(speed_y, width_y - 1, 0))
            )
        )
        first = lane == 0
        last = lane == depth_z - 1
        rate = split(0.5 * (jnp.where(first, 0.0, pltpu.roll(speed_z, 1, 1)) + speed_z))
        lower_z_rate = (jnp.where(first, 0.0, rate[0]), rate[1])
        rate = split(
            0.5 * (speed_z + jnp.where(last, 0.0, pltpu.roll(speed_z, depth_z - 1, 1)))
        )
        upper_z_rate = (rate[0], jnp.where(last, 0.0, rate[1]))
        drift = (1.5 * speed_x, 1.5 * speed_y, 1.5 * speed_z)
        upper_x = []
        for field in range(2):
            state = [state_ref[field * 8 + corner, x] for corner in range(8)]
            result = list(state)

            def update(low, high, low_flux, high_flux, d):
                both = low_flux + high_flux
                flow = drift[d] * (state[low] + state[high])
                result[low] = result[low] + ((both + low_flux) - flow)
                result[high] = result[high] + (flow - (both + high_flux))

            for k in range(4):
                low, high = k, k + 4
                across = (
                    above_x(field * 4 + k)
                    if x == width_x - 1
                    else state_ref[field * 8 + k, x + 1]
                )
                flux = upper_x_rate[0] * state[high] + upper_x_rate[1] * across
                upper_x.append(flux)
                update(low, high, lower_x[field * 4 + k], flux, 0)
            for a in range(2):
                for c in range(2):
                    low = a * 4 + c
                    high = low + 2
                    k = field * 4 + a * 2 + c
                    left = jnp.where(row == 0, below_y(k, x), pltpu.roll(state[high], 1, 0))
                    right = jnp.where(
                        row == width_y - 1,
                        above_y(k, x),
                        pltpu.roll(state[low], width_y - 1, 0),
                    )
                    update(
                        low,
                        high,
                        lower_y_rate[0] * left + lower_y_rate[1] * state[low],
                        upper_y_rate[0] * state[high] + upper_y_rate[1] * right,
                        1,
                    )
            for k in range(4):
                low, high = 2 * k, 2 * k + 1
                left = pltpu.roll(state[high], 1, 1)
                right = pltpu.roll(state[low], depth_z - 1, 1)
                update(
                    low,
                    high,
                    lower_z_rate[0] * left + lower_z_rate[1] * state[low],
                    upper_z_rate[0] * state[high] + upper_z_rate[1] * right,
                    2,
                )
            for corner in range(8):
                out_ref[field * 8 + corner, x] = result[corner]
        lower_x = upper_x
    half = lax.broadcasted_iota(jnp.int32, goal_ref.shape, 1) < depth_z // 2
    goal_ref[...] = jnp.where(half, targets_ref[:, 0:1], targets_ref[:, 1:2])
    place = index_y
    owners_row, blocks_row = owners_ref[...], blocks_ref[...]
    rows = out_ref.reshape(16 * width_x * width_y, depth_z)
    owners = [owners_row[0, entry] for entry in range(entries)]
    for entry in range(entries):
        slot = jnp.int32(0)
        for earlier in range(entry):
            slot = slot + jnp.where(owners[earlier] == owners[entry], 1, 0)
        if count_py & (count_py - 1) == 0:
            hop = owners[entry] ^ place
        else:
            hop = lax.rem(owners[entry] - place + count_py, count_py)
        sending[hop * capacity + slot] = rows[
            pl.ds(blocks_row[0, entry], 16, stride=width_x * width_y), :
        ]
    for hop in range(count_py):
        send_refs[hop][...] = sending[pl.ds(hop * capacity, capacity)]


def folded(totals):
    rows = [jnp.sum(total, axis=0, keepdims=True) for total in totals]
    depth = rows[0].shape[1]
    rows = [row + pltpu.roll(row, depth // 2, 1) for row in rows]
    half = lax.broadcasted_iota(jnp.int32, rows[0].shape, 1) < depth // 2
    return jnp.where(half, rows[0], rows[1])


def remap_call(state, relative, halos, blocks, owners, targets, count_py):
    sizes = state.shape[1:]
    _, _, depth_z = sizes
    entries = blocks.shape[1]
    capacity = max(2, 2 * entries // count_py)
    return pl.pallas_call(
        functools.partial(remap_kernel, sizes, count_py, entries, capacity),
        out_shape=(shape_of(16, *sizes), shape_of(1, depth_z))
        + (shape_of(capacity, 16, depth_z),) * count_py,
        in_specs=[in_vmem()] * 9,
        out_specs=(in_vmem(),) * (2 + count_py),
        scratch_shapes=[
            pltpu.VMEM((count_py * capacity, 16, depth_z), jnp.float32),
        ],
        compiler_params=kernel_options(),
        name="remap",
    )(state, relative, *halos, blocks, owners, targets.reshape(1, 2))


def finish_kernel(total_nodes, count_py, capacity, state_ref, total_ref, goal_ref, *refs):
    chunk_refs = refs[:count_py]
    fixed_hbm, handed_hbm, fixed_ref, handed_ref, sems = refs[count_py:]
    total = jnp.sum(total_ref[...], axis=0)
    half = lax.broadcasted_iota(jnp.int32, total.shape, 1) < total.shape[1] // 2
    sums = (
        jnp.sum(jnp.where(half, total, 0.0), axis=1, keepdims=True),
        jnp.sum(jnp.where(half, 0.0, total), axis=1, keepdims=True),
    )
    means = jnp.where(half, sums[0], sums[1]) / total_nodes
    scale = goal_ref[...] / means
    other = pltpu.roll(scale, scale.shape[1] // 2, 1)
    factors = (jnp.where(half, scale, other), jnp.where(half, other, scale))
    copies = []
    for field in range(2):
        part = pl.ds(field * 8, 8)
        fixed_ref[part] = state_ref[part] * factors[field]
        copies.append(pltpu.make_async_copy(fixed_ref.at[part], fixed_hbm.at[part], sems.at[field]))
        copies[-1].start()
    place = lax.axis_index("py")
    for hop in range(count_py):
        start = giver_of(place, hop, count_py) * capacity
        for field in range(2):
            part = pl.ds(field * 8, 8)
            handed_ref[pl.ds(start, capacity), part, :] = (
                chunk_refs[hop][:, part, :] * factors[field]
            )
    copies.append(pltpu.make_async_copy(handed_ref, handed_hbm, sems.at[2]))
    copies[-1].start()
    for copy in copies:
        copy.wait()


def finish_call(state, gathered, goal, chunks, total_nodes):
    count_py = len(chunks)
    capacity = chunks[0].shape[0]
    handed = (count_py * capacity,) + chunks[0].shape[1:]
    return pl.pallas_call(
        functools.partial(finish_kernel, total_nodes, count_py, capacity),
        out_shape=(shape_of(*state.shape), shape_of(*handed)),
        in_specs=[in_vmem()] * (3 + count_py),
        out_specs=(in_place(),) * 2,
        scratch_shapes=[
            pltpu.VMEM(state.shape, jnp.float32),
            pltpu.VMEM(handed, jnp.float32),
            pltpu.SemaphoreType.DMA((3,)),
        ],
        compiler_params=kernel_options(),
        name="finish",
    )(state, gathered, goal, *chunks)


def hop_pairs(size, hop):
    if size & (size - 1) == 0:
        return [(i, i ^ hop) for i in range(size)]
    return [(i, (i + hop) % size) for i in range(size)]


def step(conserved, velocity, targets, handoff_blocks, handoff_owner):
    count_px = lax.axis_size("px")
    count_py = lax.axis_size("py")
    device_count = count_px * count_py
    total_nodes = 8.0 * math.prod(conserved.shape[4:]) * device_count
    state, relative, xa, xb, ya, yb, total = lagrange_call(conserved, velocity, device_count)
    counts = (count_px, count_py)
    halos = []
    for message, axis, first in ((xa, 0, 0), (xb, 0, 1), (ya, 1, 0), (yb, 1, 1)):
        halos.append(lax.ppermute(message, ("px", "py"), exchanges(counts, axis, first)))
    gathered = lax.all_to_all(total, ("px", "py"), 0, 0, tiled=True)
    remapped, goal, *chunks = remap_call(
        state,
        relative,
        halos,
        handoff_blocks,
        handoff_owner.reshape(handoff_blocks.shape),
        targets,
        count_py,
    )
    received = [chunks[0]]
    for hop in range(1, count_py):
        received.append(lax.ppermute(chunks[hop], "py", hop_pairs(count_py, hop)))
    fixed, handed = finish_call(remapped, gathered, goal, received, total_nodes)
    return fixed.reshape(conserved.shape), handed[None]


def solution(mesh):
    return jax.shard_map(
        step,
        mesh=mesh,
        in_specs=(
            P(None, None, None, None, "px", "py", None),
            P(None, None, None, None, "px", "py", None),
            P(),
            P("px", "py"),
            P("px", "py", None),
        ),
        out_specs=(P(None, None, None, None, "px", "py", None), P("px", "py", None, None)),
        check_vma=False,
    )
```

```python
import functools
import math

import jax
import jax.numpy as jnp
from jax import lax
from jax.experimental import pallas as pl
from jax.experimental.pallas import tpu as pltpu
from jax.sharding import PartitionSpec as P


gamma_less = 0.4
force_step = 0.02
gauss_offset = 0.5 / math.sqrt(3.0)


def in_vmem():
    return pl.BlockSpec(memory_space=pltpu.VMEM)


def in_place():
    return pl.BlockSpec(memory_space=pltpu.HBM)


def shape_of(*shape):
    return jax.ShapeDtypeStruct(shape, jnp.float32)


def kernel_options():
    return pltpu.CompilerParams(vmem_limit_bytes=16 * 1024 * 1024)


def exchanges(counts, axis, first):
    pairs = []
    for i in range(counts[0]):
        for j in range(counts[1]):
            place = [i, j]
            partner = list(place)
            along_axis = place[axis] + 1 if (place[axis] - first) % 2 == 0 else place[axis] - 1
            if 0 <= along_axis < counts[axis]:
                partner[axis] = along_axis
            elif place[1 - axis] ^ 1 < counts[1 - axis]:
                partner[1 - axis] = place[1 - axis] ^ 1
            pairs.append((i * counts[1] + j, partner[0] * counts[1] + partner[1]))
    return pairs


def swaps(size):
    return [(i, i ^ 1 if i ^ 1 < size else i) for i in range(size)]


def giver_of(index, hop, size):
    if size & (size - 1) == 0:
        return index ^ hop
    return lax.rem(index + size - hop, size)


def lifted(low, high, value):
    middle = 0.5 * (low + high)
    tilt = value * (low - high)
    return middle + tilt, middle - tilt


def along(values, direction, operation):
    stride = (4, 2, 1)[direction]
    out = [None] * 8
    for low in range(8):
        if not low & stride:
            out[low], out[low + stride] = operation(values[low], values[low + stride])
    return out


def added(values):
    while len(values) > 1:
        values = [values[i] + values[i + 1] for i in range(0, len(values) - 1, 2)] + (
            [values[-1]] if len(values) % 2 else []
        )
    return values[0]


def quadratic_values(first, second, third):
    middle = (1.0 / 6.0) * (first + third) + (2.0 / 3.0) * second
    tilt = gauss_offset * (third - first)
    return middle - tilt, middle + tilt


def quadratic_slopes(first, second, third):
    rise = third - first
    bend = (4.0 * gauss_offset) * ((first + third) - 2.0 * second)
    return rise - bend, rise + bend


def lagrange_kernel(
    sizes,
    conserved_ref,
    velocity_ref,
    state_ref,
    relative_ref,
    xa_ref,
    xb_ref,
    ya_ref,
    yb_ref,
    total_ref,
    motion_ref,
    state_sem,
    motion_sem,
):
    width_x, width_y, depth_z = sizes
    copies = []
    for x in range(width_x):
        copies.append(
            (
                pltpu.make_async_copy(
                    conserved_ref.at[:, x], state_ref.at[:, x], state_sem.at[x]
                ),
                pltpu.make_async_copy(
                    velocity_ref.at[:, x], motion_ref.at[:, x], motion_sem.at[x]
                ),
            )
        )
    for state_copy, motion_copy in copies:
        state_copy.start()
        motion_copy.start()
    lane = lax.broadcasted_iota(jnp.int32, (width_y, depth_z), 1)
    row = lax.broadcasted_iota(jnp.int32, (width_y, depth_z), 0)
    index_x, index_y = lax.axis_index("px"), lax.axis_index("py")
    first_y = jnp.logical_and(row == 0, index_y == 0)
    last_y = jnp.logical_and(row == width_y - 1, index_y == lax.axis_size("py") - 1)
    totals = [None, None]
    for x in range(width_x):
        copies[x][0].wait()
        copies[x][1].wait()
        divergence = [None] * 8
        motion = []
        for component in range(3):

            def node(a, b, c):
                return motion_ref[component * 27 + a * 9 + b * 3 + c, x]

            total = None
            stage = {}
            for a in range(3):
                for b in range(3):
                    line = [node(a, b, c) for c in range(3)]
                    part = (line[0] + line[1]) + line[2]
                    total = part if total is None else total + part
                    rule = quadratic_slopes if component == 2 else quadratic_values
                    stage[a, b, 0], stage[a, b, 1] = rule(*line)
            second = {}
            for a in range(3):
                for c in range(2):
                    rule = quadratic_slopes if component == 1 else quadratic_values
                    second[a, 0, c], second[a, 1, c] = rule(
                        stage[a, 0, c], stage[a, 1, c], stage[a, 2, c]
                    )
            for b in range(2):
                for c in range(2):
                    rule = quadratic_slopes if component == 0 else quadratic_values
                    pair = rule(second[0, b, c], second[1, b, c], second[2, b, c])
                    for a in range(2):
                        point = a * 4 + b * 2 + c
                        divergence[point] = (
                            pair[a] if component == 0 else divergence[point] + pair[a]
                        )
            mean = total * (1.0 / 27.0)
            before = jnp.where(lane == 0, 0.0, pltpu.roll(mean, 1, 1))
            after = jnp.where(lane == depth_z - 1, 0.0, pltpu.roll(mean, depth_z - 1, 1))
            motion.append(mean - 0.25 * ((before + 2.0 * mean) + after))
            relative_ref[component, x] = motion[component]
        energy = [state_ref[8 + corner, x] for corner in range(8)]
        work = energy
        for direction in range(3):
            work = along(work, direction, lambda p, q: lifted(p, q, gauss_offset))
        work = [(gamma_less * work[point]) * divergence[point] for point in range(8)]
        for direction in range(3):
            work = along(work, direction, lambda p, q: lifted(p, q, 3.0 * gauss_offset))
        energy = [energy[corner] - force_step * work[corner] for corner in range(8)]
        for corner in range(8):
            state_ref[8 + corner, x] = energy[corner]
        half_motion = [0.5 * speed for speed in motion]
        entering = [
            jnp.where(index_x == 0, jnp.minimum(half_motion[0], 0.0), 0.0) if x == 0 else None,
            jnp.where(first_y, jnp.minimum(half_motion[1], 0.0), 0.0),
            jnp.where(lane == 0, jnp.minimum(half_motion[2], 0.0), 0.0),
        ]
        leaving = [
            jnp.where(index_x == lax.axis_size("px") - 1, jnp.maximum(half_motion[0], 0.0), 0.0)
            if x == width_x - 1
            else None,
            jnp.where(last_y, jnp.maximum(half_motion[1], 0.0), 0.0),
            jnp.where(lane == depth_z - 1, jnp.maximum(half_motion[2], 0.0), 0.0),
        ]
        for field in range(2):
            values = energy if field else [state_ref[corner, x] for corner in range(8)]
            part = None
            for direction in range(3):
                stride = (4, 2, 1)[direction]
                low = added([values[k] for k in range(8) if not k & stride])
                high = added([values[k] for k in range(8) if k & stride])
                if part is None:
                    part = low + high
                if entering[direction] is not None:
                    part = part + entering[direction] * low
                if leaving[direction] is not None:
                    part = part - leaving[direction] * high
            totals[field] = part if totals[field] is None else totals[field] + part
    total_ref[...] = jnp.broadcast_to(folded(totals)[None], total_ref.shape)
    odd_x = lax.rem(index_x, 2)
    for out_ref, side in ((xa_ref, 1 - odd_x), (xb_ref, odd_x)):
        place = side * (width_x - 1)
        for field in range(2):
            for k in range(4):
                out_ref[field * 4 + k] = state_ref[field * 8 + side * 4 + k, place]
        out_ref[8] = relative_ref[0, place]
    odd_y = lax.rem(index_y, 2)
    state_rows = state_ref.reshape(16 * width_x * width_y, depth_z)
    relative_rows = relative_ref.reshape(3 * width_x * width_y, depth_z)
    column = width_x * width_y
    for out_ref, side in ((ya_ref, 1 - odd_y), (yb_ref, odd_y)):
        place = side * (width_y - 1)
        for field in range(2):
            for a in range(2):
                for c in range(2):
                    start = (field * 8 + a * 4 + c) * column + side * 2 * column + place
                    out_ref[field * 4 + a * 2 + c] = state_rows[
                        pl.ds(start, width_x, stride=width_y), :
                    ]
        out_ref[8] = relative_rows[pl.ds(column + place, width_x, stride=width_y), :]


def lagrange_call(conserved, velocity, device_count):
    width_x, width_y, depth_z = conserved.shape[4:]
    sizes = (width_x, width_y, depth_z)
    return pl.pallas_call(
        functools.partial(lagrange_kernel, sizes),
        out_shape=(
            shape_of(16, *sizes),
            shape_of(3, *sizes),
            shape_of(9, width_y, depth_z),
            shape_of(9, width_y, depth_z),
            shape_of(9, width_x, depth_z),
            shape_of(9, width_x, depth_z),
            shape_of(device_count, 1, depth_z),
        ),
        in_specs=[in_place()] * 2,
        out_specs=(in_vmem(),) * 7,
        scratch_shapes=[
            pltpu.VMEM((81,) + sizes, jnp.float32),
            pltpu.SemaphoreType.DMA((width_x,)),
            pltpu.SemaphoreType.DMA((width_x,)),
        ],
        compiler_params=kernel_options(),
        name="lagrange",
    )(
        pltpu.with_memory_space_constraint(conserved.reshape((16,) + sizes), pltpu.HBM),
        pltpu.with_memory_space_constraint(velocity.reshape((81,) + sizes), pltpu.HBM),
    )


def remap_kernel(
    sizes,
    count_py,
    entries,
    capacity,
    state_ref,
    relative_ref,
    xa_ref,
    xb_ref,
    ya_ref,
    yb_ref,
    blocks_ref,
    owners_ref,
    targets_ref,
    *refs,
):
    width_x, width_y, depth_z = sizes
    out_ref, goal_ref = refs[:2]
    send_refs = refs[2 : 2 + count_py]
    (sending,) = refs[2 + count_py :]
    lane = lax.broadcasted_iota(jnp.int32, (width_y, depth_z), 1)
    row = lax.broadcasted_iota(jnp.int32, (width_y, depth_z), 0)
    index_x = lax.axis_index("px")
    index_y = lax.axis_index("py")
    even_x = lax.rem(index_x, 2) == 0
    even_y = lax.rem(index_y, 2) == 0
    some_below_x, some_above_x = index_x > 0, index_x < lax.axis_size("px") - 1
    some_below_y, some_above_y = index_y > 0, index_y < count_py - 1

    def below_x(k):
        return jnp.where(some_below_x, jnp.where(even_x, xb_ref[k], xa_ref[k]), 0.0)

    def above_x(k):
        return jnp.where(some_above_x, jnp.where(even_x, xa_ref[k], xb_ref[k]), 0.0)

    def below_y(k, x):
        ya, yb = ya_ref[k, pl.ds(x, 1), :], yb_ref[k, pl.ds(x, 1), :]
        return jnp.where(some_below_y, jnp.where(even_y, yb, ya), 0.0)

    def above_y(k, x):
        ya, yb = ya_ref[k, pl.ds(x, 1), :], yb_ref[k, pl.ds(x, 1), :]
        return jnp.where(some_above_y, jnp.where(even_y, ya, yb), 0.0)

    def split(speed):
        return jnp.maximum(speed, 0.0), jnp.minimum(speed, 0.0)

    sending[...] = jnp.zeros(sending.shape, jnp.float32)
    speed = relative_ref[0, 0]
    coefficient = split(0.5 * (below_x(8) + speed))
    lower_x = [
        coefficient[0] * below_x(field * 4 + k) + coefficient[1] * state_ref[field * 8 + k, 0]
        for field in range(2)
        for k in range(4)
    ]
    for x in range(width_x):
        speed_x, speed_y, speed_z = (relative_ref[d, x] for d in range(3))
        beyond = above_x(8) if x == width_x - 1 else relative_ref[0, x + 1]
        upper_x_rate = split(0.5 * (speed_x + beyond))
        y_below, y_above = below_y(8, x), above_y(8, x)
        lower_y_rate = split(
            0.5 * (jnp.where(row == 0, y_below, pltpu.roll(speed_y, 1, 0)) + speed_y)
        )
        upper_y_rate = split(
            0.5
            * (
                speed_y
                + jnp.where(row == width_y - 1, y_above, pltpu.roll(speed_y, width_y - 1, 0))
            )
        )
        first = lane == 0
        last = lane == depth_z - 1
        rate = split(0.5 * (jnp.where(first, 0.0, pltpu.roll(speed_z, 1, 1)) + speed_z))
        lower_z_rate = (jnp.where(first, 0.0, rate[0]), rate[1])
        rate = split(
            0.5 * (speed_z + jnp.where(last, 0.0, pltpu.roll(speed_z, depth_z - 1, 1)))
        )
        upper_z_rate = (rate[0], jnp.where(last, 0.0, rate[1]))
        drift = (1.5 * speed_x, 1.5 * speed_y, 1.5 * speed_z)
        upper_x = []
        for field in range(2):
            state = [state_ref[field * 8 + corner, x] for corner in range(8)]
            result = list(state)

            def update(low, high, low_flux, high_flux, d):
                both = low_flux + high_flux
                flow = drift[d] * (state[low] + state[high])
                result[low] = result[low] + ((both + low_flux) - flow)
                result[high] = result[high] + (flow - (both + high_flux))

            for k in range(4):
                low, high = k, k + 4
                across = (
                    above_x(field * 4 + k)
                    if x == width_x - 1
                    else state_ref[field * 8 + k, x + 1]
                )
                flux = upper_x_rate[0] * state[high] + upper_x_rate[1] * across
                upper_x.append(flux)
                update(low, high, lower_x[field * 4 + k], flux, 0)
            for a in range(2):
                for c in range(2):
                    low = a * 4 + c
                    high = low + 2
                    k = field * 4 + a * 2 + c
                    left = jnp.where(row == 0, below_y(k, x), pltpu.roll(state[high], 1, 0))
                    right = jnp.where(
                        row == width_y - 1,
                        above_y(k, x),
                        pltpu.roll(state[low], width_y - 1, 0),
                    )
                    update(
                        low,
                        high,
                        lower_y_rate[0] * left + lower_y_rate[1] * state[low],
                        upper_y_rate[0] * state[high] + upper_y_rate[1] * right,
                        1,
                    )
            for k in range(4):
                low, high = 2 * k, 2 * k + 1
                left = pltpu.roll(state[high], 1, 1)
                right = pltpu.roll(state[low], depth_z - 1, 1)
                update(
                    low,
                    high,
                    lower_z_rate[0] * left + lower_z_rate[1] * state[low],
                    upper_z_rate[0] * state[high] + upper_z_rate[1] * right,
                    2,
                )
            for corner in range(8):
                out_ref[field * 8 + corner, x] = result[corner]
        lower_x = upper_x
    half = lax.broadcasted_iota(jnp.int32, goal_ref.shape, 1) < depth_z // 2
    goal_ref[...] = jnp.where(half, targets_ref[:, 0:1], targets_ref[:, 1:2])
    place = index_y
    owners_row, blocks_row = owners_ref[...], blocks_ref[...]
    rows = out_ref.reshape(16 * width_x * width_y, depth_z)
    owners = [owners_row[0, entry] for entry in range(entries)]
    for entry in range(entries):
        slot = jnp.int32(0)
        for earlier in range(entry):
            slot = slot + jnp.where(owners[earlier] == owners[entry], 1, 0)
        if count_py & (count_py - 1) == 0:
            hop = owners[entry] ^ place
        else:
            hop = lax.rem(owners[entry] - place + count_py, count_py)
        sending[hop * capacity + slot] = rows[
            pl.ds(blocks_row[0, entry], 16, stride=width_x * width_y), :
        ]
    for hop in range(count_py):
        send_refs[hop][...] = sending[pl.ds(hop * capacity, capacity)]


def folded(totals):
    rows = [jnp.sum(total, axis=0, keepdims=True) for total in totals]
    depth = rows[0].shape[1]
    rows = [row + pltpu.roll(row, depth // 2, 1) for row in rows]
    half = lax.broadcasted_iota(jnp.int32, rows[0].shape, 1) < depth // 2
    return jnp.where(half, rows[0], rows[1])


def remap_call(state, relative, halos, blocks, owners, targets, count_py):
    sizes = state.shape[1:]
    _, _, depth_z = sizes
    entries = blocks.shape[1]
    capacity = max(2, 2 * entries // count_py)
    return pl.pallas_call(
        functools.partial(remap_kernel, sizes, count_py, entries, capacity),
        out_shape=(shape_of(16, *sizes), shape_of(1, depth_z))
        + (shape_of(capacity, 16, depth_z),) * count_py,
        in_specs=[in_vmem()] * 9,
        out_specs=(in_vmem(),) * (2 + count_py),
        scratch_shapes=[
            pltpu.VMEM((count_py * capacity, 16, depth_z), jnp.float32),
        ],
        compiler_params=kernel_options(),
        name="remap",
    )(state, relative, *halos, blocks, owners, targets.reshape(1, 2))


def finish_kernel(total_nodes, count_py, capacity, state_ref, total_ref, goal_ref, *refs):
    chunk_refs = refs[:count_py]
    fixed_hbm, handed_hbm, fixed_ref, handed_ref, sems = refs[count_py:]
    total = jnp.sum(total_ref[...], axis=0)
    half = lax.broadcasted_iota(jnp.int32, total.shape, 1) < total.shape[1] // 2
    sums = (
        jnp.sum(jnp.where(half, total, 0.0), axis=1, keepdims=True),
        jnp.sum(jnp.where(half, 0.0, total), axis=1, keepdims=True),
    )
    means = jnp.where(half, sums[0], sums[1]) / total_nodes
    scale = goal_ref[...] / means
    other = pltpu.roll(scale, scale.shape[1] // 2, 1)
    factors = (jnp.where(half, scale, other), jnp.where(half, other, scale))
    copies = []
    for field in range(2):
        part = pl.ds(field * 8, 8)
        fixed_ref[part] = state_ref[part] * factors[field]
        copies.append(pltpu.make_async_copy(fixed_ref.at[part], fixed_hbm.at[part], sems.at[field]))
        copies[-1].start()
    place = lax.axis_index("py")
    for hop in range(count_py):
        start = giver_of(place, hop, count_py) * capacity
        for field in range(2):
            part = pl.ds(field * 8, 8)
            handed_ref[pl.ds(start, capacity), part, :] = (
                chunk_refs[hop][:, part, :] * factors[field]
            )
    copies.append(pltpu.make_async_copy(handed_ref, handed_hbm, sems.at[2]))
    copies[-1].start()
    for copy in copies:
        copy.wait()


def finish_call(state, gathered, goal, chunks, total_nodes):
    count_py = len(chunks)
    capacity = chunks[0].shape[0]
    handed = (count_py * capacity,) + chunks[0].shape[1:]
    return pl.pallas_call(
        functools.partial(finish_kernel, total_nodes, count_py, capacity),
        out_shape=(shape_of(*state.shape), shape_of(*handed)),
        in_specs=[in_vmem()] * (3 + count_py),
        out_specs=(in_place(),) * 2,
        scratch_shapes=[
            pltpu.VMEM(state.shape, jnp.float32),
            pltpu.VMEM(handed, jnp.float32),
            pltpu.SemaphoreType.DMA((3,)),
        ],
        compiler_params=kernel_options(),
        name="finish",
    )(state, gathered, goal, *chunks)


def hop_pairs(size, hop):
    if size & (size - 1) == 0:
        return [(i, i ^ hop) for i in range(size)]
    return [(i, (i + hop) % size) for i in range(size)]


def step(conserved, velocity, targets, handoff_blocks, handoff_owner):
    count_px = lax.axis_size("px")
    count_py = lax.axis_size("py")
    device_count = count_px * count_py
    total_nodes = 8.0 * math.prod(conserved.shape[4:]) * device_count
    state, relative, xa, xb, ya, yb, total = lagrange_call(conserved, velocity, device_count)
    counts = (count_px, count_py)
    halos = []
    for message, axis, first in ((xa, 0, 0), (xb, 0, 1), (ya, 1, 0), (yb, 1, 1)):
        halos.append(lax.ppermute(message, ("px", "py"), exchanges(counts, axis, first)))
    total = lax.ppermute(total, "py", swaps(count_py))
    gathered = lax.all_to_all(total, ("px", "py"), 0, 0, tiled=True)
    remapped, goal, *chunks = remap_call(
        state,
        relative,
        halos,
        handoff_blocks,
        handoff_owner.reshape(handoff_blocks.shape),
        targets,
        count_py,
    )
    received = [chunks[0]]
    for hop in range(1, count_py):
        received.append(lax.ppermute(chunks[hop], "py", hop_pairs(count_py, hop)))
    fixed, handed = finish_call(remapped, gathered, goal, received, total_nodes)
    return fixed.reshape(conserved.shape), handed[None]


def solution(mesh):
    return jax.shard_map(
        step,
        mesh=mesh,
        in_specs=(
            P(None, None, None, None, "px", "py", None),
            P(None, None, None, None, "px", "py", None),
            P(),
            P("px", "py"),
            P("px", "py", None),
        ),
        out_specs=(P(None, None, None, None, "px", "py", None), P("px", "py", None, None)),
        check_vma=False,
    )
```

```python
import functools
import math

import jax
import jax.numpy as jnp
from jax import lax
from jax.experimental import pallas as pl
from jax.experimental.pallas import tpu as pltpu
from jax.sharding import PartitionSpec as P


gamma_less = 0.4
force_step = 0.02
gauss_offset = 0.5 / math.sqrt(3.0)


def in_vmem():
    return pl.BlockSpec(memory_space=pltpu.VMEM)


def in_place():
    return pl.BlockSpec(memory_space=pltpu.HBM)


def shape_of(*shape):
    return jax.ShapeDtypeStruct(shape, jnp.float32)


def kernel_options():
    return pltpu.CompilerParams(vmem_limit_bytes=16 * 1024 * 1024)


def exchanges(counts, axis, first):
    pairs = []
    for i in range(counts[0]):
        for j in range(counts[1]):
            place = [i, j]
            partner = list(place)
            along_axis = place[axis] + 1 if (place[axis] - first) % 2 == 0 else place[axis] - 1
            if 0 <= along_axis < counts[axis]:
                partner[axis] = along_axis
            elif place[1 - axis] ^ 1 < counts[1 - axis]:
                partner[1 - axis] = place[1 - axis] ^ 1
            pairs.append((i * counts[1] + j, partner[0] * counts[1] + partner[1]))
    return pairs


def swaps(size):
    return [(i, i ^ 1 if i ^ 1 < size else i) for i in range(size)]


def giver_of(index, hop, size):
    if size & (size - 1) == 0:
        return index ^ hop
    return lax.rem(index + size - hop, size)


def lifted(low, high, value):
    middle = 0.5 * (low + high)
    tilt = value * (low - high)
    return middle + tilt, middle - tilt


def along(values, direction, operation):
    stride = (4, 2, 1)[direction]
    out = [None] * 8
    for low in range(8):
        if not low & stride:
            out[low], out[low + stride] = operation(values[low], values[low + stride])
    return out


def added(values):
    while len(values) > 1:
        values = [values[i] + values[i + 1] for i in range(0, len(values) - 1, 2)] + (
            [values[-1]] if len(values) % 2 else []
        )
    return values[0]


def quadratic_values(first, second, third):
    middle = (1.0 / 6.0) * (first + third) + (2.0 / 3.0) * second
    tilt = gauss_offset * (third - first)
    return middle - tilt, middle + tilt


def quadratic_slopes(first, second, third):
    rise = third - first
    bend = (4.0 * gauss_offset) * ((first + third) - 2.0 * second)
    return rise - bend, rise + bend


def lagrange_kernel(
    sizes,
    conserved_ref,
    velocity_ref,
    state_ref,
    relative_ref,
    xa_ref,
    xb_ref,
    ya_ref,
    yb_ref,
    total_ref,
    motion_ref,
    state_sem,
    motion_sem,
):
    width_x, width_y, depth_z = sizes
    copies = []
    for x in range(width_x):
        copies.append(
            (
                pltpu.make_async_copy(
                    conserved_ref.at[:, x], state_ref.at[:, x], state_sem.at[x]
                ),
                pltpu.make_async_copy(
                    velocity_ref.at[:, x], motion_ref.at[:, x], motion_sem.at[x]
                ),
            )
        )
    for state_copy, motion_copy in copies:
        state_copy.start()
        motion_copy.start()
    lane = lax.broadcasted_iota(jnp.int32, (width_y, depth_z), 1)
    row = lax.broadcasted_iota(jnp.int32, (width_y, depth_z), 0)
    index_x, index_y = lax.axis_index("px"), lax.axis_index("py")
    first_y = jnp.logical_and(row == 0, index_y == 0)
    last_y = jnp.logical_and(row == width_y - 1, index_y == lax.axis_size("py") - 1)
    totals = [None, None]
    for x in range(width_x):
        copies[x][0].wait()
        copies[x][1].wait()
        divergence = [None] * 8
        motion = []
        for component in range(3):

            def node(a, b, c):
                return motion_ref[component * 27 + a * 9 + b * 3 + c, x]

            total = None
            stage = {}
            for a in range(3):
                for b in range(3):
                    line = [node(a, b, c) for c in range(3)]
                    part = (line[0] + line[1]) + line[2]
                    total = part if total is None else total + part
                    rule = quadratic_slopes if component == 2 else quadratic_values
                    stage[a, b, 0], stage[a, b, 1] = rule(*line)
            second = {}
            for a in range(3):
                for c in range(2):
                    rule = quadratic_slopes if component == 1 else quadratic_values
                    second[a, 0, c], second[a, 1, c] = rule(
                        stage[a, 0, c], stage[a, 1, c], stage[a, 2, c]
                    )
            for b in range(2):
                for c in range(2):
                    rule = quadratic_slopes if component == 0 else quadratic_values
                    pair = rule(second[0, b, c], second[1, b, c], second[2, b, c])
                    for a in range(2):
                        point = a * 4 + b * 2 + c
                        divergence[point] = (
                            pair[a] if component == 0 else divergence[point] + pair[a]
                        )
            mean = total * (1.0 / 27.0)
            before = jnp.where(lane == 0, 0.0, pltpu.roll(mean, 1, 1))
            after = jnp.where(lane == depth_z - 1, 0.0, pltpu.roll(mean, depth_z - 1, 1))
            motion.append(mean - 0.25 * ((before + 2.0 * mean) + after))
            relative_ref[component, x] = motion[component]
        energy = [state_ref[8 + corner, x] for corner in range(8)]
        work = energy
        for direction in range(3):
            work = along(work, direction, lambda p, q: lifted(p, q, gauss_offset))
        work = [(gamma_less * work[point]) * divergence[point] for point in range(8)]
        for direction in range(3):
            work = along(work, direction, lambda p, q: lifted(p, q, 3.0 * gauss_offset))
        energy = [energy[corner] - force_step * work[corner] for corner in range(8)]
        for corner in range(8):
            state_ref[8 + corner, x] = energy[corner]
        half_motion = [0.5 * speed for speed in motion]
        entering = [
            jnp.where(index_x == 0, jnp.minimum(half_motion[0], 0.0), 0.0) if x == 0 else None,
            jnp.where(first_y, jnp.minimum(half_motion[1], 0.0), 0.0),
            jnp.where(lane == 0, jnp.minimum(half_motion[2], 0.0), 0.0),
        ]
        leaving = [
            jnp.where(index_x == lax.axis_size("px") - 1, jnp.maximum(half_motion[0], 0.0), 0.0)
            if x == width_x - 1
            else None,
            jnp.where(last_y, jnp.maximum(half_motion[1], 0.0), 0.0),
            jnp.where(lane == depth_z - 1, jnp.maximum(half_motion[2], 0.0), 0.0),
        ]
        for field in range(2):
            values = energy if field else [state_ref[corner, x] for corner in range(8)]
            part = None
            for direction in range(3):
                stride = (4, 2, 1)[direction]
                low = added([values[k] for k in range(8) if not k & stride])
                high = added([values[k] for k in range(8) if k & stride])
                if part is None:
                    part = low + high
                if entering[direction] is not None:
                    part = part + entering[direction] * low
                if leaving[direction] is not None:
                    part = part - leaving[direction] * high
            totals[field] = part if totals[field] is None else totals[field] + part
    total_ref[...] = jnp.broadcast_to(folded(totals)[None], total_ref.shape)
    odd_x = lax.rem(index_x, 2)
    for out_ref, side in ((xa_ref, 1 - odd_x), (xb_ref, odd_x)):
        place = side * (width_x - 1)
        for field in range(2):
            for k in range(4):
                out_ref[field * 4 + k] = state_ref[field * 8 + side * 4 + k, place]
        out_ref[8] = relative_ref[0, place]
    odd_y = lax.rem(index_y, 2)
    state_rows = state_ref.reshape(16 * width_x * width_y, depth_z)
    relative_rows = relative_ref.reshape(3 * width_x * width_y, depth_z)
    column = width_x * width_y
    for out_ref, side in ((ya_ref, 1 - odd_y), (yb_ref, odd_y)):
        place = side * (width_y - 1)
        for field in range(2):
            for a in range(2):
                for c in range(2):
                    start = (field * 8 + a * 4 + c) * column + side * 2 * column + place
                    out_ref[field * 4 + a * 2 + c] = state_rows[
                        pl.ds(start, width_x, stride=width_y), :
                    ]
        out_ref[8] = relative_rows[pl.ds(column + place, width_x, stride=width_y), :]


def lagrange_call(conserved, velocity, device_count):
    width_x, width_y, depth_z = conserved.shape[4:]
    sizes = (width_x, width_y, depth_z)
    return pl.pallas_call(
        functools.partial(lagrange_kernel, sizes),
        out_shape=(
            shape_of(16, *sizes),
            shape_of(3, *sizes),
            shape_of(9, width_y, depth_z),
            shape_of(9, width_y, depth_z),
            shape_of(9, width_x, depth_z),
            shape_of(9, width_x, depth_z),
            shape_of(device_count, 1, depth_z),
        ),
        in_specs=[in_place()] * 2,
        out_specs=(in_vmem(),) * 7,
        scratch_shapes=[
            pltpu.VMEM((81,) + sizes, jnp.float32),
            pltpu.SemaphoreType.DMA((width_x,)),
            pltpu.SemaphoreType.DMA((width_x,)),
        ],
        compiler_params=kernel_options(),
        name="lagrange",
    )(
        pltpu.with_memory_space_constraint(conserved.reshape((16,) + sizes), pltpu.HBM),
        pltpu.with_memory_space_constraint(velocity.reshape((81,) + sizes), pltpu.HBM),
    )


def remap_kernel(
    sizes,
    count_py,
    entries,
    capacity,
    state_ref,
    relative_ref,
    xa_ref,
    xb_ref,
    ya_ref,
    yb_ref,
    blocks_ref,
    owners_ref,
    targets_ref,
    *refs,
):
    width_x, width_y, depth_z = sizes
    out_ref, goal_ref = refs[:2]
    send_refs = refs[2 : 2 + count_py]
    (sending,) = refs[2 + count_py :]
    lane = lax.broadcasted_iota(jnp.int32, (width_y, depth_z), 1)
    row = lax.broadcasted_iota(jnp.int32, (width_y, depth_z), 0)
    index_x = lax.axis_index("px")
    index_y = lax.axis_index("py")
    even_x = lax.rem(index_x, 2) == 0
    even_y = lax.rem(index_y, 2) == 0
    some_below_x, some_above_x = index_x > 0, index_x < lax.axis_size("px") - 1
    some_below_y, some_above_y = index_y > 0, index_y < count_py - 1

    def below_x(k):
        return jnp.where(some_below_x, jnp.where(even_x, xb_ref[k], xa_ref[k]), 0.0)

    def above_x(k):
        return jnp.where(some_above_x, jnp.where(even_x, xa_ref[k], xb_ref[k]), 0.0)

    def below_y(k, x):
        ya, yb = ya_ref[k, pl.ds(x, 1), :], yb_ref[k, pl.ds(x, 1), :]
        return jnp.where(some_below_y, jnp.where(even_y, yb, ya), 0.0)

    def above_y(k, x):
        ya, yb = ya_ref[k, pl.ds(x, 1), :], yb_ref[k, pl.ds(x, 1), :]
        return jnp.where(some_above_y, jnp.where(even_y, ya, yb), 0.0)

    def split(speed):
        return jnp.maximum(speed, 0.0), jnp.minimum(speed, 0.0)

    sending[...] = jnp.zeros(sending.shape, jnp.float32)
    speed = relative_ref[0, 0]
    coefficient = split(0.5 * (below_x(8) + speed))
    lower_x = [
        coefficient[0] * below_x(field * 4 + k) + coefficient[1] * state_ref[field * 8 + k, 0]
        for field in range(2)
        for k in range(4)
    ]
    for x in range(width_x):
        speed_x, speed_y, speed_z = (relative_ref[d, x] for d in range(3))
        beyond = above_x(8) if x == width_x - 1 else relative_ref[0, x + 1]
        upper_x_rate = split(0.5 * (speed_x + beyond))
        y_below, y_above = below_y(8, x), above_y(8, x)
        lower_y_rate = split(
            0.5 * (jnp.where(row == 0, y_below, pltpu.roll(speed_y, 1, 0)) + speed_y)
        )
        upper_y_rate = split(
            0.5
            * (
                speed_y
                + jnp.where(row == width_y - 1, y_above, pltpu.roll(speed_y, width_y - 1, 0))
            )
        )
        first = lane == 0
        last = lane == depth_z - 1
        rate = split(0.5 * (jnp.where(first, 0.0, pltpu.roll(speed_z, 1, 1)) + speed_z))
        lower_z_rate = (jnp.where(first, 0.0, rate[0]), rate[1])
        rate = split(
            0.5 * (speed_z + jnp.where(last, 0.0, pltpu.roll(speed_z, depth_z - 1, 1)))
        )
        upper_z_rate = (rate[0], jnp.where(last, 0.0, rate[1]))
        drift = (1.5 * speed_x, 1.5 * speed_y, 1.5 * speed_z)
        upper_x = []
        for field in range(2):
            state = [state_ref[field * 8 + corner, x] for corner in range(8)]
            result = list(state)

            def update(low, high, low_flux, high_flux, d):
                both = low_flux + high_flux
                flow = drift[d] * (state[low] + state[high])
                result[low] = result[low] + ((both + low_flux) - flow)
                result[high] = result[high] + (flow - (both + high_flux))

            for k in range(4):
                low, high = k, k + 4
                across = (
                    above_x(field * 4 + k)
                    if x == width_x - 1
                    else state_ref[field * 8 + k, x + 1]
                )
                flux = upper_x_rate[0] * state[high] + upper_x_rate[1] * across
                upper_x.append(flux)
                update(low, high, lower_x[field * 4 + k], flux, 0)
            for a in range(2):
                for c in range(2):
                    low = a * 4 + c
                    high = low + 2
                    k = field * 4 + a * 2 + c
                    left = jnp.where(row == 0, below_y(k, x), pltpu.roll(state[high], 1, 0))
                    right = jnp.where(
                        row == width_y - 1,
                        above_y(k, x),
                        pltpu.roll(state[low], width_y - 1, 0),
                    )
                    update(
                        low,
                        high,
                        lower_y_rate[0] * left + lower_y_rate[1] * state[low],
                        upper_y_rate[0] * state[high] + upper_y_rate[1] * right,
                        1,
                    )
            for k in range(4):
                low, high = 2 * k, 2 * k + 1
                left = pltpu.roll(state[high], 1, 1)
                right = pltpu.roll(state[low], depth_z - 1, 1)
                update(
                    low,
                    high,
                    lower_z_rate[0] * left + lower_z_rate[1] * state[low],
                    upper_z_rate[0] * state[high] + upper_z_rate[1] * right,
                    2,
                )
            for corner in range(8):
                out_ref[field * 8 + corner, x] = result[corner]
        lower_x = upper_x
    half = lax.broadcasted_iota(jnp.int32, goal_ref.shape, 1) < depth_z // 2
    goal_ref[...] = jnp.where(half, targets_ref[:, 0:1], targets_ref[:, 1:2])
    place = index_y
    owners_row, blocks_row = owners_ref[...], blocks_ref[...]
    rows = out_ref.reshape(16 * width_x * width_y, depth_z)
    owners = [owners_row[0, entry] for entry in range(entries)]
    for entry in range(entries):
        slot = jnp.int32(0)
        for earlier in range(entry):
            slot = slot + jnp.where(owners[earlier] == owners[entry], 1, 0)
        if count_py & (count_py - 1) == 0:
            hop = owners[entry] ^ place
        else:
            hop = lax.rem(owners[entry] - place + count_py, count_py)
        sending[hop * capacity + slot] = rows[
            pl.ds(blocks_row[0, entry], 16, stride=width_x * width_y), :
        ]
    for hop in range(count_py):
        send_refs[hop][...] = sending[pl.ds(hop * capacity, capacity)]


def folded(totals):
    rows = [jnp.sum(total, axis=0, keepdims=True) for total in totals]
    depth = rows[0].shape[1]
    rows = [row + pltpu.roll(row, depth // 2, 1) for row in rows]
    half = lax.broadcasted_iota(jnp.int32, rows[0].shape, 1) < depth // 2
    return jnp.where(half, rows[0], rows[1])


def remap_call(state, relative, halos, blocks, owners, targets, count_py):
    sizes = state.shape[1:]
    _, _, depth_z = sizes
    entries = blocks.shape[1]
    capacity = max(2, 2 * entries // count_py)
    return pl.pallas_call(
        functools.partial(remap_kernel, sizes, count_py, entries, capacity),
        out_shape=(shape_of(16, *sizes), shape_of(1, depth_z))
        + (shape_of(capacity, 16, depth_z),) * count_py,
        in_specs=[in_vmem()] * 9,
        out_specs=(in_vmem(),) * (2 + count_py),
        scratch_shapes=[
            pltpu.VMEM((count_py * capacity, 16, depth_z), jnp.float32),
        ],
        compiler_params=kernel_options(),
        name="remap",
    )(state, relative, *halos, blocks, owners, targets.reshape(1, 2))


def finish_kernel(total_nodes, count_py, capacity, state_ref, total_ref, goal_ref, *refs):
    chunk_refs = refs[:count_py]
    fixed_ref, handed_ref = refs[count_py:]
    total = jnp.sum(total_ref[...], axis=0)
    half = lax.broadcasted_iota(jnp.int32, total.shape, 1) < total.shape[1] // 2
    sums = (
        jnp.sum(jnp.where(half, total, 0.0), axis=1, keepdims=True),
        jnp.sum(jnp.where(half, 0.0, total), axis=1, keepdims=True),
    )
    means = jnp.where(half, sums[0], sums[1]) / total_nodes
    scale = goal_ref[...] / means
    other = pltpu.roll(scale, scale.shape[1] // 2, 1)
    factors = (jnp.where(half, scale, other), jnp.where(half, other, scale))
    for field in range(2):
        part = pl.ds(field * 8, 8)
        fixed_ref[part] = state_ref[part] * factors[field]
    place = lax.axis_index("py")
    for hop in range(count_py):
        start = giver_of(place, hop, count_py) * capacity
        for field in range(2):
            part = pl.ds(field * 8, 8)
            handed_ref[pl.ds(start, capacity), part, :] = (
                chunk_refs[hop][:, part, :] * factors[field]
            )


def finish_call(state, gathered, goal, chunks, total_nodes):
    count_py = len(chunks)
    capacity = chunks[0].shape[0]
    handed = (count_py * capacity,) + chunks[0].shape[1:]
    return pl.pallas_call(
        functools.partial(finish_kernel, total_nodes, count_py, capacity),
        out_shape=(shape_of(*state.shape), shape_of(*handed)),
        in_specs=[in_vmem()] * (3 + count_py),
        out_specs=(in_vmem(),) * 2,
        compiler_params=kernel_options(),
        name="finish",
    )(state, gathered, goal, *chunks)


def hop_pairs(size, hop):
    if size & (size - 1) == 0:
        return [(i, i ^ hop) for i in range(size)]
    return [(i, (i + hop) % size) for i in range(size)]


def step(conserved, velocity, targets, handoff_blocks, handoff_owner):
    count_px = lax.axis_size("px")
    count_py = lax.axis_size("py")
    device_count = count_px * count_py
    total_nodes = 8.0 * math.prod(conserved.shape[4:]) * device_count
    state, relative, xa, xb, ya, yb, total = lagrange_call(conserved, velocity, device_count)
    counts = (count_px, count_py)
    halos = []
    for message, axis, first in ((xa, 0, 0), (xb, 0, 1), (ya, 1, 0), (yb, 1, 1)):
        halos.append(lax.ppermute(message, ("px", "py"), exchanges(counts, axis, first)))
    total = lax.ppermute(total, "py", swaps(count_py))
    gathered = lax.all_to_all(total, ("px", "py"), 0, 0, tiled=True)
    remapped, goal, *chunks = remap_call(
        state,
        relative,
        halos,
        handoff_blocks,
        handoff_owner.reshape(handoff_blocks.shape),
        targets,
        count_py,
    )
    received = [chunks[0]]
    for hop in range(1, count_py):
        received.append(lax.ppermute(chunks[hop], "py", hop_pairs(count_py, hop)))
    fixed, handed = finish_call(remapped, gathered, goal, received, total_nodes)
    return fixed.reshape(conserved.shape), handed[None]


def solution(mesh):
    return jax.shard_map(
        step,
        mesh=mesh,
        in_specs=(
            P(None, None, None, None, "px", "py", None),
            P(None, None, None, None, "px", "py", None),
            P(),
            P("px", "py"),
            P("px", "py", None),
        ),
        out_specs=(P(None, None, None, None, "px", "py", None), P("px", "py", None, None)),
        check_vma=False,
    )
```
